32 devices in a mesh: ord: 4 (over x, core), blk: 8 (over z, y).
Axes of the slice: x: 2, y: 2, z: 4, core: 2. Of those that a mesh axis runs over, the one named last changes fastest.
Arguments:
- coefficients: bfloat16 [32, 2, 256, 4096], P('ord', None, None, 'blk'), may hold values from -1.0546875 to 1.0546875
- leaf_factors: bfloat16 [32, 128, 4096], P('ord', None, 'blk'), may hold values from -0.25 to 0.25
- level_interpolants: bfloat16 [3, 2, 32, 128, 1024], P(None, None, 'ord', None, 'blk'), may hold values from -0.375 to 0.375
- latitude_factors: bfloat16 [32, 5120, 128], P('ord', 'blk'), may hold values from -0.5 to 0.5
- order_ids: int32 [32], replicated, may hold values from 0 to 8191, as said below
Outputs:
- products: bfloat16 [256, 128, 5120], P(None, 'ord', 'blk')
The draws below stay inside these ranges and needn't reach their ends.
Inputs may be any that keep to these rules, and one draw needn't show every extreme that they name: `order_ids`: the slots hold distinct orders of the truncation.
All inputs are finite; a program needn't handle non-finite values.
Results may differ from the reference program's by a relative error of at most 0.011.
Values may be sent and summed in bfloat16 or wider, within the bound.
A program may use at most 128 MiB of HBM per device.

```python
import math
import jax
import jax.numpy as jnp
import numpy as np
from jax import lax

FIELDS = 256
LEAF = 512
RANK = 128
PERIOD = 16384
ORDER_RANGE = 8192
NLON = 256
LEVELS = 3
LAT_DEV = 640
ORDERS = 32
DEGREES = 4096
LATS = 5120
BLK_RANKS = 1024
PAIRS = 128
N_BLK = 8


def draw_order_ids(key, part):
    selected_block = jax.random.permutation(jax.random.fold_in(key, 7), ORDER_RANGE)
    return selected_block[:ORDERS].astype(jnp.int32)


def shard_levels(rng, shape, split, smallest, largest):
    level = 1.0
    for position, blocks in split:
        draws = jax.random.uniform(jax.random.fold_in(jax.random.fold_in(rng, 6), position), (blocks,), jnp.float32, smallest / len(split), largest / len(split))
        level = level * jnp.repeat(jnp.exp(draws), shape[position] // blocks).reshape((-1,) + (1,) * (len(shape) - 1 - position))
    return level


def scatter_about(rng, extent, deviation, bound, split=(), kind=jnp.bfloat16):
    values = jax.random.normal(rng, extent, jnp.float32) * deviation
    if len(split) > 0:
        values = shard_levels(rng, extent, split, -0.22, 0.18) * values
    return jnp.clip(values, min=-bound, max=bound).astype(kind)


def setup_inputs(seed: int = 0) -> dict:
    key_list = jax.random.split(jax.random.key(seed), 6)
    coefficients = scatter_about(key_list[0], (ORDERS, 2, FIELDS, DEGREES), (0.5 * ORDERS ** -0.5), 1.0546875, ((0, 4), (3, 8)))
    leaf_factors = scatter_about(key_list[1], (ORDERS, RANK, DEGREES), LEAF ** -0.5, 0.25, ((0, 4), (2, 8)))
    level_interpolants = scatter_about(key_list[2], (LEVELS, 2, ORDERS, RANK, BLK_RANKS), (2 * RANK) ** -0.5, 0.375, ((2, 4), (4, 8)))
    latitude_factors = scatter_about(key_list[3], (ORDERS, LATS, RANK), RANK ** -0.5, 0.5, ((0, 4), (1, 8)))
    order_ids = draw_order_ids(jax.random.fold_in(key_list[5], 71), 0)
    return {"coefficients": coefficients, "leaf_factors": leaf_factors, "level_interpolants": level_interpolants, "latitude_factors": latitude_factors, "order_ids": order_ids}


def synthesis_table(order_ids, count, period):
    steps = jnp.arange(count, dtype=jnp.int32)
    phase = ((order_ids[:, None].astype(jnp.int32) * steps[None, :]) % period).astype(jnp.float32) * (2.0 * math.pi / period)
    weight = jnp.where(order_ids == 0, 1.0, 2.0).astype(jnp.float32)[:, None]
    table = jnp.stack([weight * jnp.cos(phase), -weight * jnp.sin(phase)], axis=1)
    return table.astype(jnp.bfloat16)


def reference(coefficients, leaf_factors, level_interpolants, latitude_factors, order_ids):
    partner_lists = [np.arange(N_BLK) ^ (N_BLK >> (k + 1)) for k in range(LEVELS)]

    def per_order(items):
        coef, leafm, levm = items
        flat = coef.astype(jnp.float32).reshape(2 * FIELDS, N_BLK, LEAF)
        leaves = leafm.astype(jnp.float32).reshape(RANK, N_BLK, LEAF)
        combined_sum = jnp.einsum('cjl,rjl->cjr', flat, leaves).astype(jnp.bfloat16)
        levels = levm.astype(jnp.float32).reshape(LEVELS, 2, RANK, N_BLK, RANK)
        for k in range(LEVELS):
            partner_block = combined_sum[:, partner_lists[k], :]
            mixed = jnp.einsum('cjr,sjr->cjs', combined_sum.astype(jnp.float32), levels[k, 0])
            mixed = mixed + jnp.einsum('cjr,sjr->cjs', partner_block.astype(jnp.float32), levels[k, 1])
            combined_sum = mixed.astype(jnp.bfloat16)
        return combined_sum

    combined_sum = lax.map(per_order, (coefficients, leaf_factors, jnp.moveaxis(level_interpolants, 2, 0)))
    table = synthesis_table(order_ids, NLON, PERIOD).astype(jnp.float32)
    by_block = jnp.moveaxis(combined_sum, 2, 0)
    lat_blocks = jnp.moveaxis(latitude_factors.reshape(ORDERS, N_BLK, LAT_DEV, RANK), 1, 0)

    def per_block(items):
        red, lat = items
        values = jnp.einsum('mcr,mlr->mcl', red.astype(jnp.float32), lat.astype(jnp.float32))
        values = values.astype(jnp.bfloat16).reshape(ORDERS, 2, FIELDS, LAT_DEV)
        grid = jnp.einsum('mrk,mrfl->kfl', table, values.astype(jnp.float32))
        grid = grid.reshape(NLON, PAIRS, 2, LAT_DEV)
        return (grid[:, :, 0, :] * grid[:, :, 1, :]).astype(jnp.bfloat16)

    block_list = lax.map(per_block, (by_block, lat_blocks))
    return jnp.transpose(block_list, (1, 2, 0, 3)).reshape(NLON, PAIRS, LATS)
```

```python
import functools
import math

import jax
import jax.numpy as jnp
from jax import lax
from jax.experimental import pallas as pl
from jax.experimental.pallas import tpu as pltpu
from jax.sharding import PartitionSpec as P

PERIOD = 16384
NLON = 256
LANES = 128
FIELDS = 16
ROWS = 2 * FIELDS
QUAD = 4
WINDOW = 4
LEVEL_LAG = 3
BATCH = 2
FIRST_UNIT = 20
UNIT_DELAY = 17
MIB = 2**20
MESH = pl.DeviceIdType.MESH
NT = (((1,), (1,)), ((), ()))


def iota(shape, dimension):
    return lax.broadcasted_iota(jnp.int32, shape, dimension)


def synthesis_table(order_ids, count, period):
    steps = iota((count, order_ids.shape[1]), 0)
    phase = lax.rem(steps * order_ids, period).astype(jnp.float32) * (2.0 * math.pi / period)
    weight = jnp.where(order_ids == 0, 1.0, 2.0).astype(jnp.float32)
    table = jnp.concatenate([weight * jnp.cos(phase), -weight * jnp.sin(phase)], axis=1)
    return table.astype(jnp.bfloat16)


def spread_tables(order_ids, wide_ref):
    total = order_ids.shape[1]
    table = synthesis_table(order_ids, NLON, PERIOD)
    tall, broad = wide_ref.shape[1:]
    row, column = iota((2 * total, broad), 0), iota((2 * total, broad), 1)
    source = ((column >> 2) & 1) * total + (column >> 3)
    columns = (row == source).astype(jnp.float32).astype(jnp.bfloat16)
    step = min(tall, 256)
    for side in range(2):
        for r in range(0, tall, step):
            row, lon = iota((step, NLON), 0) + r, iota((step, NLON), 1)
            rows = (((row >> 2) ^ side) == lon).astype(jnp.float32).astype(jnp.bfloat16)
            some = jnp.dot(rows, table, preferred_element_type=jnp.float32).astype(jnp.bfloat16)
            most = jnp.dot(some, columns, preferred_element_type=jnp.float32)
            keep = (iota((step, broad), 0) & 3) == (iota((step, broad), 1) & 3)
            wide_ref[side, pl.ds(r, step), :] = jnp.where(keep, most, 0.0).astype(jnp.bfloat16)


def row_order():
    size = 128
    to, come = iota((size, size), 0), iota((size, size), 1)
    inside = to & 31
    block, parity, part, pair = inside >> 4, (inside >> 3) & 1, (inside >> 2) & 1, inside & 3
    source = (to - inside) + part * FIELDS + block * 8 + pair * 2 + parity
    return (source == come).astype(jnp.float32).astype(jnp.bfloat16)


def products_unit(rows, lat, wide, values, first, f, t, store):
    total = rows.shape[1]
    nil = jnp.zeros((ROWS, rows.shape[3]), jnp.bfloat16)

    @pl.loop(0, total // 2, unroll=16)
    def _(m):
        both = jnp.concatenate(
            [
                jnp.concatenate([rows[f, 2 * m], nil], axis=1),
                jnp.concatenate([nil, rows[f, 2 * m + 1]], axis=1),
            ],
            axis=0,
        )
        factors = jnp.concatenate([lat[t, 2 * m], lat[t, 2 * m + 1]], axis=1)
        mapped = lax.dot_general(both, factors, NT, preferred_element_type=jnp.float32)
        at = pl.ds(pl.multiple_of(m * 16, 16), 16)
        for q in range(4):
            values[q // 2, at, (q % 2) * LANES : (q % 2 + 1) * LANES] = jnp.concatenate(
                [mapped[8 * q : 8 * q + 8], mapped[ROWS + 8 * q : ROWS + 8 * q + 8]], axis=0
            ).astype(jnp.bfloat16)

    tall = wide.shape[1]
    step = 256
    low = iota((step // 8, 8, LANES), 1) < QUAD
    for r in range(0, tall, step):
        grid = jnp.dot(wide[0, r : r + step], values[0], preferred_element_type=jnp.float32)
        first[r : r + step] = grid[:, :LANES] * grid[:, LANES:]
    for r in range(0, tall, step):
        grid = jnp.dot(wide[1, r : r + step], values[1], preferred_element_type=jnp.float32)
        here = (grid[:, :LANES] * grid[:, LANES:]).reshape(step // 8, 8, LANES)
        there = first[r : r + step].reshape(step // 8, 8, LANES)
        even = jnp.where(low, there, here)
        odd = pltpu.roll(jnp.where(low, here, there), QUAD, 1)
        mixed = jnp.concatenate([even[:, None], odd[:, None]], axis=1)
        store(r // QUAD, step // QUAD, mixed.reshape(step // QUAD, 8, LANES).astype(jnp.bfloat16))


def butterfly_kernel(
    n_ord, n_blk, early, coef_hbm, leaf_hbm, interp_hbm, lat_hbm, ids_hbm, *refs,
):
    if early:
        rows, lat, wide, done, half, *refs = refs
    else:
        rows, lat, wide, *refs = refs
    (
        coef, leaf, interp, ids, own, last, came, values, first,
        coef_sem, leaf_sem, interp_sem, ids_sem, lat_in_sem,
        level_send, level_recv, group_send, group_recv, own_sem,
        lat_send, lat_recv, lat_pass,
    ) = refs
    me_ord, me_blk = lax.axis_index("ord"), lax.axis_index("blk")
    pieces, orders, _, parts, _, depth = coef.shape
    levels = interp.shape[0]
    chunks = pieces * orders
    tiles = lat.shape[0]
    height = n_ord * ROWS
    rank = interp.shape[-1]
    steps = chunks + LEVEL_LAG * (levels - 1)

    def coef_in(f, i, part):
        return pltpu.make_async_copy(
            coef_hbm.at[i, part, :, pl.ds(pl.multiple_of(f * FIELDS, FIELDS), FIELDS)],
            coef.at[f, i, :, part], coef_sem.at[f, i, part],
        )

    def leaf_in(i):
        return pltpu.make_async_copy(leaf_hbm.at[i], leaf.at[i], leaf_sem.at[i])

    interp_in = pltpu.make_async_copy(interp_hbm, interp, interp_sem)
    ids_in = pltpu.make_async_copy(ids_hbm, ids, ids_sem)

    def lat_rows(t, o):
        return lat.at[t, pl.ds(pl.multiple_of(o * orders, orders), orders)]

    def lat_in(t):
        return pltpu.make_async_copy(
            lat_hbm.at[:, pl.ds(t * LANES, LANES)], lat_rows(t, me_ord), lat_in_sem.at[t]
        )

    for i in range(orders):
        leaf_in(i).start()
        for part in range(parts):
            coef_in(0, i, part).start()
        if i == 1:
            lat_in(0).start()
            ids_in.start()
            interp_in.start()
    for t in range(1, tiles):
        lat_in(t).start()

    barrier = pltpu.get_barrier_semaphore()
    partners = [me_blk ^ (n_blk >> (k + 1)) for k in range(levels)]
    for k in range(levels):
        pl.semaphore_signal(barrier, inc=1, device_id={"blk": partners[k]}, device_id_type=MESH)
    for d in range(1, n_ord):
        pl.semaphore_signal(
            barrier, inc=1, device_id={"ord": lax.rem(me_ord + d, n_ord)}, device_id_type=MESH
        )

    def leaf_step(c):
        f, i = c // orders, lax.rem(c, orders)

        @pl.when(f == 0)
        def _():
            leaf_in(i).wait()

        for part in range(parts):
            coef_in(f, i, part).wait()
        reduced = lax.dot_general(
            coef[f, i].reshape(height, depth), leaf[i], NT, preferred_element_type=jnp.float32
        ).astype(jnp.bfloat16)
        order = row_order()
        for r in range(0, height, 128):
            own[0, c, r : r + 128] = jnp.dot(
                order, reduced[r : r + 128], preferred_element_type=jnp.float32
            ).astype(jnp.bfloat16)

    leaf_step(0)
    pl.semaphore_wait(barrier, levels + n_ord - 1)

    def level_copy(k, c):
        return pltpu.make_async_remote_copy(
            src_ref=own.at[k, c], dst_ref=came.at[k, c],
            send_sem=level_send.at[k, c], recv_sem=level_recv.at[k, c],
            device_id={"blk": partners[k]}, device_id_type=MESH,
        )

    batches = orders // BATCH

    def landing(b):
        at = me_ord * orders + lax.rem(b, batches) * BATCH
        return rows.at[b // batches, pl.ds(at, BATCH)]

    def group_copy(b, d):
        peer = lax.rem(me_ord + d, n_ord)
        return pltpu.make_async_remote_copy(
            src_ref=last.at[b, peer], dst_ref=landing(b),
            send_sem=group_send.at[b, d], recv_sem=group_recv.at[b, d],
            device_id={"ord": peer}, device_id_type=MESH,
        )

    def own_copy(b):
        return pltpu.make_async_copy(last.at[b, me_ord], landing(b), own_sem.at[b])

    spans = n_ord // 2
    mate = me_ord ^ 1

    def lat_copy(d, t):
        target = mate if d == 0 else lax.rem(me_ord + 2 * d, n_ord)
        return pltpu.make_async_remote_copy(
            src_ref=lat_rows(t, me_ord), dst_ref=lat_rows(t, me_ord),
            send_sem=lat_send.at[d, t], recv_sem=lat_recv.at[d, t],
            device_id={"ord": target}, device_id_type=MESH,
        )

    def lat_forward(d, t):
        source = lax.rem(me_ord + n_ord - 2 * d, n_ord)
        return pltpu.make_async_remote_copy(
            src_ref=lat_rows(t, source), dst_ref=lat_rows(t, source),
            send_sem=lat_pass.at[d, t], recv_sem=lat_recv.at[spans + d, t],
            device_id={"ord": mate}, device_id_type=MESH,
        )

    def lat_start(t):
        lat_in(t).wait()
        for d in range(spans - 1, -1, -1):
            lat_copy(d, t).start()

    def lat_pass_on(t):
        for d in range(1, spans):
            lat_copy(d, t).wait_recv()
            lat_forward(d, t).start()

    def lat_arrived(t):
        lat_copy(0, t).wait_recv()
        for d in range(1, spans):
            lat_forward(d, t).wait_recv()

    def rows_arrived(f):
        @pl.loop(0, batches)
        def _(b):
            for d in range(1, n_ord):
                group_copy(f * batches + b, d).wait_recv()
            own_copy(f * batches + b).wait()

    level_copy(0, 0).start()

    @pl.loop(1, WINDOW)
    def _(c):
        leaf_step(c)
        level_copy(0, c).start()

    for t in range(min(2, tiles)):
        lat_start(t)
    for f in range(1, pieces):
        @pl.loop(0, orders)
        def _(i):
            for part in range(parts):
                coef_in(f, i, part).start()
    ids_in.wait()
    spread_tables(ids[...], wide)
    interp_in.wait()

    def level_step(k, c, after):
        i = lax.rem(c, orders)
        level_copy(k, c).wait_recv()
        after()
        mixed = lax.dot_general(
            own[k, c], interp[k, 0, i], NT, preferred_element_type=jnp.float32
        ) + lax.dot_general(
            came[k, c], interp[k, 1, i], NT, preferred_element_type=jnp.float32
        )
        mixed = mixed.astype(jnp.bfloat16)
        if k + 1 < levels:
            own[k + 1, c] = mixed
            level_copy(k + 1, c).start()
        else:
            b = c // BATCH
            last[b, :, lax.rem(c, BATCH)] = mixed.reshape(n_ord, ROWS, rank)

            @pl.when(lax.rem(c, BATCH) == BATCH - 1)
            def _():
                for d in range(1, n_ord):
                    group_copy(b, d).start()
                own_copy(b).start()

    begins = []
    for f in range(pieces - 1):
        begins.append(max(FIRST_UNIT + f * tiles, f * orders + UNIT_DELAY))

    if early:
        half[...] = jnp.zeros(half.shape, half.dtype)

    @pl.loop(0, steps)
    def _(s):
        @pl.when(s + WINDOW < chunks)
        def _():
            leaf_step(s + WINDOW)

        for k in range(levels):
            c = s - k * LEVEL_LAG

            def after():
                if k == 0:
                    @pl.when(s + WINDOW < chunks)
                    def _():
                        level_copy(0, s + WINDOW).start()

            @pl.when((c >= 0) & (c < chunks))
            def _():
                level_step(k, c, after)

        for t in range(2, tiles):
            @pl.when(s == min(3 * (t - 1), steps - 1))
            def _():
                lat_start(t)

        for t in range(tiles):
            @pl.when(s == min(4 * t + 6, steps - 1))
            def _():
                lat_pass_on(t)

        if early:
            f = sum((s >= b).astype(jnp.int32) for b in begins) - 1
            begin = begins[0]
            for before, b in zip(begins, begins[1:]):
                begin = begin + (s >= b).astype(jnp.int32) * (b - before)
            t = s - begin

            @pl.when((f >= 0) & (t < tiles))
            def _():
                @pl.when(f == 0)
                def _():
                    lat_arrived(t)

                @pl.when(t == 0)
                def _():
                    rows_arrived(f)

                lanes = pl.ds(pl.multiple_of(t * LANES, LANES), LANES)

                def store(at, count, mixed):
                    where = pl.ds(at, count)
                    done[f // 2, where, :, lanes] = jnp.concatenate(
                        [half[where, :, lanes], mixed], axis=1
                    )
                    half[where, :, lanes] = mixed

                products_unit(rows, lat, wide, values, first, f, t, store)

    if not early:
        for t in range(tiles):
            lat_arrived(t)
    rows_arrived(pieces - 1)

    for t in range(tiles):
        for d in range(spans):
            lat_copy(d, t).wait_send()
        for d in range(1, spans):
            lat_forward(d, t).wait_send()

    @pl.loop(0, chunks)
    def _(c):
        for k in range(levels):
            level_copy(k, c).wait_send()

    @pl.loop(0, chunks // BATCH)
    def _(b):
        for d in range(1, n_ord):
            group_copy(b, d).wait_send()


def butterfly(coefficients, leaf_factors, interpolants, latitude_factors, order_ids, n_ord, n_blk):
    orders, parts, fields, depth = coefficients.shape
    rank = leaf_factors.shape[1]
    levels = interpolants.shape[0]
    lats = latitude_factors.shape[1]
    tiles = lats // LANES
    group = fields // n_ord
    pieces = group // FIELDS
    chunks = pieces * orders
    total = n_ord * orders
    spans = n_ord // 2
    early = pieces > 1
    height = n_ord * ROWS
    hbm_spec = pl.BlockSpec(memory_space=pltpu.HBM)
    vmem_spec = pl.BlockSpec(memory_space=pltpu.VMEM)
    dma = pltpu.SemaphoreType.DMA
    bf16 = jnp.bfloat16
    out_shape = [
        pltpu.VMEM((pieces, total, ROWS, rank), bf16),
        pltpu.VMEM((tiles, total, LANES, rank), bf16),
        pltpu.VMEM((2, QUAD * NLON, 8 * total), bf16),
    ]
    if early:
        out_shape += [
            pltpu.VMEM((pieces // 2, NLON, 16, lats), bf16),
            pltpu.VMEM((NLON, 8, lats), bf16),
        ]
    coefficients = coefficients.reshape(orders, parts, n_ord, group, depth)
    hold = functools.partial(pltpu.with_memory_space_constraint, memory_space=pltpu.HBM)
    return pl.pallas_call(
        functools.partial(butterfly_kernel, n_ord, n_blk, early),
        out_shape=tuple(out_shape),
        in_specs=[hbm_spec] * 5,
        out_specs=tuple([vmem_spec] * len(out_shape)),
        scratch_shapes=[
            pltpu.VMEM((pieces, orders, n_ord, parts, FIELDS, depth), bf16),
            pltpu.VMEM(leaf_factors.shape, bf16),
            pltpu.VMEM(interpolants.shape, bf16),
            pltpu.VMEM((1, total), jnp.int32),
            pltpu.VMEM((levels, chunks, height, rank), bf16),
            pltpu.VMEM((chunks // BATCH, n_ord, BATCH, ROWS, rank), bf16),
            pltpu.VMEM((levels, chunks, height, rank), bf16),
            pltpu.VMEM((2, 8 * total, 2 * LANES), bf16),
            pltpu.VMEM((QUAD * NLON, LANES), jnp.float32),
            dma((pieces, orders, parts)),
            dma((orders,)),
            dma,
            dma,
            dma((tiles,)),
            dma((levels, chunks)),
            dma((levels, chunks)),
            dma((chunks // BATCH, n_ord)),
            dma((chunks // BATCH, n_ord)),
            dma((chunks // BATCH,)),
            dma((spans, tiles)),
            dma((2 * spans, tiles)),
            dma((spans, tiles)),
        ],
        compiler_params=pltpu.CompilerParams(
            collective_id=0, has_side_effects=True, vmem_limit_bytes=24 * MIB
        ),
        name="butterfly",
    )(
        hold(coefficients), hold(leaf_factors), hold(interpolants), hold(latitude_factors),
        hold(order_ids[None, :]),
    )


def products_kernel(early, rows, lat, wide, *refs):
    if early:
        done, half, out, values, first, stage, done_sem, stage_sem = refs
    else:
        out, values, first, stage, stage_sem = refs
    pieces = rows.shape[0]
    tiles = lat.shape[0]
    deep = stage.shape[2]
    pairs = out.shape[1]
    whole = pairs // deep - 1

    def done_out(h):
        return pltpu.make_async_copy(
            done.at[h], out.at[:, pl.ds(h * deep, deep)], done_sem.at[h]
        )

    def stage_out(t):
        lanes = pl.ds(pl.multiple_of(t * LANES, LANES), LANES)
        return pltpu.make_async_copy(
            stage.at[t], out.at[:, pl.ds(whole * deep, deep), lanes], stage_sem.at[t]
        )

    for h in range(whole):
        done_out(h).start()

    @pl.loop(0, tiles)
    def _(t):
        lanes = pl.ds(pl.multiple_of(t * LANES, LANES), LANES)

        def store(at, count, mixed):
            where = pl.ds(at, count)
            if early:
                mixed = jnp.concatenate([half[where, :, lanes], mixed], axis=1)
            stage[t, where] = mixed

        products_unit(rows, lat, wide, values, first, pieces - 1, t, store)
        stage_out(t).start()

    for h in range(whole):
        done_out(h).wait()
    for t in range(tiles):
        stage_out(t).wait()


def products_of(rows, lat, wide, *more):
    pieces, total, _, rank = rows.shape
    tiles = lat.shape[0]
    early = len(more) > 0
    pairs = pieces * FIELDS // 2
    deep = 16 if early else 8
    dma = pltpu.SemaphoreType.DMA
    scratch = [
        pltpu.VMEM((2, 8 * total, 2 * LANES), jnp.bfloat16),
        pltpu.VMEM((QUAD * NLON, LANES), jnp.float32),
        pltpu.VMEM((tiles, NLON, deep, LANES), jnp.bfloat16),
    ]
    if early:
        scratch.append(dma((max(pairs // deep - 1, 1),)))
    scratch.append(dma((tiles,)))
    operands = [
        pltpu.with_memory_space_constraint(x, memory_space=pltpu.VMEM)
        for x in (rows, lat, wide, *more)
    ]
    return pl.pallas_call(
        functools.partial(products_kernel, early),
        out_shape=jax.ShapeDtypeStruct((NLON, pairs, tiles * LANES), jnp.bfloat16),
        in_specs=[pl.BlockSpec(memory_space=pltpu.VMEM)] * len(operands),
        out_specs=pl.BlockSpec(memory_space=pl.ANY),
        scratch_shapes=scratch,
        compiler_params=pltpu.CompilerParams(vmem_limit_bytes=12 * MIB),
        name="products",
    )(*operands)


def per_device(coefficients, leaf_factors, level_interpolants, latitude_factors, order_ids):
    return products_of(
        *butterfly(
            coefficients, leaf_factors, level_interpolants, latitude_factors, order_ids,
            lax.axis_size("ord"), lax.axis_size("blk"),
        )
    )


def solution(mesh):
    in_specs = (
        P("ord", None, None, "blk"),
        P("ord", None, "blk"),
        P(None, None, "ord", None, "blk"),
        P("ord", "blk", None),
        P(),
    )
    out_specs = P(None, "ord", "blk")
    return jax.shard_map(
        per_device, mesh=mesh, in_specs=in_specs, out_specs=out_specs, check_vma=False
    )
```

```python
import functools
import math

import jax
import jax.numpy as jnp
from jax import lax
from jax.experimental import pallas as pl
from jax.experimental.pallas import tpu as pltpu
from jax.sharding import PartitionSpec as P

PERIOD = 16384
NLON = 256
LANES = 128
FIELDS = 16
ROWS = 2 * FIELDS
QUAD = 4
CHUNK = 2
WINDOW = 2
LEVEL_LAG = 2
FIRST_UNIT = 23
UNIT_DELAY = 12
LAT_STEP = 2
LAT_PASS = 4
MIB = 2**20
MESH = pl.DeviceIdType.MESH
NT = (((1,), (1,)), ((), ()))


def iota(shape, dimension):
    return lax.broadcasted_iota(jnp.int32, shape, dimension)


def synthesis_table(order_ids, count, period):
    steps = iota((count, order_ids.shape[1]), 0)
    phase = lax.rem(steps * order_ids, period).astype(jnp.float32) * (2.0 * math.pi / period)
    weight = jnp.where(order_ids == 0, 1.0, 2.0).astype(jnp.float32)
    table = jnp.concatenate([weight * jnp.cos(phase), -weight * jnp.sin(phase)], axis=1)
    return table.astype(jnp.bfloat16)


def spread_tables(order_ids, wide_ref):
    total = order_ids.shape[1]
    table = synthesis_table(order_ids, NLON, PERIOD)
    tall, broad = wide_ref.shape[1:]
    row, column = iota((2 * total, broad), 0), iota((2 * total, broad), 1)
    source = ((column >> 2) & 1) * total + (column >> 3)
    columns = (row == source).astype(jnp.float32).astype(jnp.bfloat16)
    step = min(tall, 256)
    for side in range(2):
        for r in range(0, tall, step):
            row, lon = iota((step, NLON), 0) + r, iota((step, NLON), 1)
            rows = (((row >> 2) ^ side) == lon).astype(jnp.float32).astype(jnp.bfloat16)
            some = jnp.dot(rows, table, preferred_element_type=jnp.float32).astype(jnp.bfloat16)
            most = jnp.dot(some, columns, preferred_element_type=jnp.float32)
            keep = (iota((step, broad), 0) & 3) == (iota((step, broad), 1) & 3)
            wide_ref[side, pl.ds(r, step), :] = jnp.where(keep, most, 0.0).astype(jnp.bfloat16)


def row_order():
    size = 128
    to, come = iota((size, size), 0), iota((size, size), 1)
    inside = to & 31
    block, parity, part, pair = inside >> 4, (inside >> 3) & 1, (inside >> 2) & 1, inside & 3
    source = (to - inside) + part * FIELDS + block * 8 + pair * 2 + parity
    return (source == come).astype(jnp.float32).astype(jnp.bfloat16)


def products_unit(rows, lat, wide, values, first, f, t, store):
    total = rows.shape[1]
    nil = jnp.zeros((ROWS, rows.shape[3]), jnp.bfloat16)

    @pl.loop(0, total // 2, unroll=16)
    def _(m):
        both = jnp.concatenate(
            [
                jnp.concatenate([rows[f, 2 * m], nil], axis=1),
                jnp.concatenate([nil, rows[f, 2 * m + 1]], axis=1),
            ],
            axis=0,
        )
        factors = jnp.concatenate([lat[t, 2 * m], lat[t, 2 * m + 1]], axis=1)
        mapped = lax.dot_general(both, factors, NT, preferred_element_type=jnp.float32)
        at = pl.ds(pl.multiple_of(m * 16, 16), 16)
        for q in range(4):
            values[q // 2, at, (q % 2) * LANES : (q % 2 + 1) * LANES] = jnp.concatenate(
                [mapped[8 * q : 8 * q + 8], mapped[ROWS + 8 * q : ROWS + 8 * q + 8]], axis=0
            ).astype(jnp.bfloat16)

    tall = wide.shape[1]
    step = 256
    low = iota((step // 8, 8, LANES), 1) < QUAD
    for r in range(0, tall, step):
        grid = jnp.dot(wide[0, r : r + step], values[0], preferred_element_type=jnp.float32)
        first[r : r + step] = grid[:, :LANES] * grid[:, LANES:]
    for r in range(0, tall, step):
        grid = jnp.dot(wide[1, r : r + step], values[1], preferred_element_type=jnp.float32)
        here = (grid[:, :LANES] * grid[:, LANES:]).reshape(step // 8, 8, LANES)
        there = first[r : r + step].reshape(step // 8, 8, LANES)
        even = jnp.where(low, there, here)
        odd = pltpu.roll(jnp.where(low, here, there), QUAD, 1)
        mixed = jnp.concatenate([even[:, None], odd[:, None]], axis=1)
        store(r // QUAD, step // QUAD, mixed.reshape(step // QUAD, 8, LANES).astype(jnp.bfloat16))


def butterfly_kernel(
    n_ord, n_blk, early, coef_hbm, leaf_hbm, interp_hbm, lat_hbm, ids_hbm, *refs,
):
    if early:
        rows, lat, wide, done, half, *refs = refs
    else:
        rows, lat, wide, *refs = refs
    (
        coef, leaf, interp, ids, own, last, came, values, first,
        coef_sem, leaf_sem, interp_sem, ids_sem, lat_in_sem,
        level_send, level_recv, group_send, group_recv, own_sem,
        lat_send, lat_recv, lat_pass,
    ) = refs
    me_ord, me_blk = lax.axis_index("ord"), lax.axis_index("blk")
    pieces, orders, _, parts, _, depth = coef.shape
    levels = interp.shape[0]
    per_piece = orders // CHUNK
    chunks = pieces * per_piece
    tiles = lat.shape[0]
    height = n_ord * ROWS
    rank = interp.shape[-1]
    steps = chunks + LEVEL_LAG * (levels - 1)

    def coef_in(f, i, part):
        return pltpu.make_async_copy(
            coef_hbm.at[i, part, :, pl.ds(pl.multiple_of(f * FIELDS, FIELDS), FIELDS)],
            coef.at[f, i, :, part], coef_sem.at[f, i, part],
        )

    def leaf_in(i):
        return pltpu.make_async_copy(leaf_hbm.at[i], leaf.at[i], leaf_sem.at[i])

    interp_in = pltpu.make_async_copy(interp_hbm, interp, interp_sem)
    ids_in = pltpu.make_async_copy(ids_hbm, ids, ids_sem)

    def lat_rows(t, o):
        return lat.at[t, pl.ds(pl.multiple_of(o * orders, orders), orders)]

    def lat_in(t):
        return pltpu.make_async_copy(
            lat_hbm.at[:, pl.ds(t * LANES, LANES)], lat_rows(t, me_ord), lat_in_sem.at[t]
        )

    for i in range(orders):
        leaf_in(i).start()
        for part in range(parts):
            coef_in(0, i, part).start()
        if i == 1:
            lat_in(0).start()
            ids_in.start()
            interp_in.start()
    for t in range(1, tiles):
        lat_in(t).start()

    barrier = pltpu.get_barrier_semaphore()
    partners = [me_blk ^ (n_blk >> (k + 1)) for k in range(levels)]
    for k in range(levels):
        pl.semaphore_signal(barrier, inc=1, device_id={"blk": partners[k]}, device_id_type=MESH)
    for d in range(1, n_ord):
        pl.semaphore_signal(
            barrier, inc=1, device_id={"ord": lax.rem(me_ord + d, n_ord)}, device_id_type=MESH
        )

    def leaf_step(c):
        f, i = c // per_piece, lax.rem(c, per_piece) * CHUNK
        for h in range(CHUNK):
            @pl.when(f == 0)
            def _():
                leaf_in(i + h).wait()

            for part in range(parts):
                coef_in(f, i + h, part).wait()
        order = row_order()
        for h in range(CHUNK):
            reduced = lax.dot_general(
                coef[f, i + h].reshape(height, depth), leaf[i + h], NT,
                preferred_element_type=jnp.float32,
            ).astype(jnp.bfloat16)
            for r in range(0, height, 128):
                own[0, c, h, r : r + 128] = jnp.dot(
                    order, reduced[r : r + 128], preferred_element_type=jnp.float32
                ).astype(jnp.bfloat16)

    leaf_step(0)
    pl.semaphore_wait(barrier, levels + n_ord - 1)

    def level_copy(k, c):
        return pltpu.make_async_remote_copy(
            src_ref=own.at[k, c], dst_ref=came.at[k, c],
            send_sem=level_send.at[k, c], recv_sem=level_recv.at[k, c],
            device_id={"blk": partners[k]}, device_id_type=MESH,
        )

    def landing(c):
        at = me_ord * orders + lax.rem(c, per_piece) * CHUNK
        return rows.at[c // per_piece, pl.ds(at, CHUNK)]

    def group_copy(c, d):
        peer = lax.rem(me_ord + d, n_ord)
        return pltpu.make_async_remote_copy(
            src_ref=last.at[c, peer], dst_ref=landing(c),
            send_sem=group_send.at[c, d], recv_sem=group_recv.at[c, d],
            device_id={"ord": peer}, device_id_type=MESH,
        )

    def own_copy(c):
        return pltpu.make_async_copy(last.at[c, me_ord], landing(c), own_sem.at[c])

    spans = n_ord // 2
    mate = me_ord ^ 1

    def lat_copy(d, t):
        target = mate if d == 0 else lax.rem(me_ord + 2 * d, n_ord)
        return pltpu.make_async_remote_copy(
            src_ref=lat_rows(t, me_ord), dst_ref=lat_rows(t, me_ord),
            send_sem=lat_send.at[d, t], recv_sem=lat_recv.at[d, t],
            device_id={"ord": target}, device_id_type=MESH,
        )

    def lat_forward(d, t):
        source = lax.rem(me_ord + n_ord - 2 * d, n_ord)
        return pltpu.make_async_remote_copy(
            src_ref=lat_rows(t, source), dst_ref=lat_rows(t, source),
            send_sem=lat_pass.at[d, t], recv_sem=lat_recv.at[spans + d, t],
            device_id={"ord": mate}, device_id_type=MESH,
        )

    def lat_start(t):
        lat_in(t).wait()
        for d in range(spans - 1, -1, -1):
            lat_copy(d, t).start()

    def lat_pass_on(t):
        for d in range(1, spans):
            lat_copy(d, t).wait_recv()
            lat_forward(d, t).start()

    def lat_arrived(t):
        lat_copy(0, t).wait_recv()
        for d in range(1, spans):
            lat_forward(d, t).wait_recv()

    def rows_arrived(f):
        for n in range(per_piece):
            for d in range(1, n_ord):
                group_copy(f * per_piece + n, d).wait_recv()
            own_copy(f * per_piece + n).wait()

    level_copy(0, 0).start()
    for f in range(1, pieces):
        @pl.loop(0, orders)
        def _(i):
            for part in range(parts):
                coef_in(f, i, part).start()

    for c in range(1, WINDOW):
        leaf_step(c)
        level_copy(0, c).start()

    for t in range(tiles):
        lat_start(t)
    ids_in.wait()
    spread_tables(ids[...], wide)
    interp_in.wait()

    def level_step(k, s):
        c = s - k * LEVEL_LAG

        @pl.when((c >= 0) & (c < chunks))
        def _():
            i = lax.rem(c, per_piece) * CHUNK
            level_copy(k, c).wait_recv()
            if k == 0:
                @pl.when(s + WINDOW < chunks)
                def _():
                    level_copy(0, s + WINDOW).start()

            for h in range(CHUNK):
                both = jnp.concatenate([own[k, c, h], came[k, c, h]], axis=1)
                factors = jnp.concatenate([interp[k, 0, i + h], interp[k, 1, i + h]], axis=1)
                mixed = lax.dot_general(
                    both, factors, NT, preferred_element_type=jnp.float32
                ).astype(jnp.bfloat16)
                if k + 1 < levels:
                    own[k + 1, c, h] = mixed
                else:
                    last[c, :, h] = mixed.reshape(n_ord, ROWS, rank)
            if k + 1 < levels:
                level_copy(k + 1, c).start()
            else:
                for d in range(1, n_ord):
                    group_copy(c, d).start()
                own_copy(c).start()

    begins = []
    for f in range(pieces - 1):
        begins.append(max(FIRST_UNIT + f * (tiles + 1), 2 * (f * per_piece + UNIT_DELAY - 2)))

    if early:
        half[...] = jnp.zeros(half.shape, half.dtype)

    @pl.loop(0, max([2 * steps] + [b + tiles for b in begins]))
    def _(j):
        s = j // 2

        @pl.when(lax.rem(j, 2) == 0)
        def _():
            @pl.when(s + WINDOW < chunks)
            def _():
                leaf_step(s + WINDOW)

            level_step(0, s)
            for t in range(tiles):
                @pl.when(s == min(LAT_STEP * t + LAT_PASS, steps - 1))
                def _():
                    lat_pass_on(t)

        @pl.when(lax.rem(j, 2) == 1)
        def _():
            for k in range(1, levels):
                level_step(k, s)

        if early:
            f = sum((j >= b).astype(jnp.int32) for b in begins) - 1
            begin = begins[0]
            for before, b in zip(begins, begins[1:]):
                begin = begin + (j >= b).astype(jnp.int32) * (b - before)
            t = j - begin

            @pl.when((f >= 0) & (t < tiles))
            def _():
                @pl.when(f == 0)
                def _():
                    lat_arrived(t)

                @pl.when(t == 0)
                def _():
                    rows_arrived(f)

                lanes = pl.ds(pl.multiple_of(t * LANES, LANES), LANES)

                def store(at, count, mixed):
                    where = pl.ds(at, count)
                    done[f // 2, where, :, lanes] = jnp.concatenate(
                        [half[where, :, lanes], mixed], axis=1
                    )
                    half[where, :, lanes] = mixed

                products_unit(rows, lat, wide, values, first, f, t, store)

    if not early:
        for t in range(tiles):
            lat_arrived(t)
    for f in range(len(begins), pieces):
        rows_arrived(f)

    for t in range(tiles):
        for d in range(spans):
            lat_copy(d, t).wait_send()
        for d in range(1, spans):
            lat_forward(d, t).wait_send()

    @pl.loop(0, chunks)
    def _(c):
        for k in range(levels):
            level_copy(k, c).wait_send()
        for d in range(1, n_ord):
            group_copy(c, d).wait_send()


def butterfly(coefficients, leaf_factors, interpolants, latitude_factors, order_ids, n_ord, n_blk):
    orders, parts, fields, depth = coefficients.shape
    rank = leaf_factors.shape[1]
    levels = interpolants.shape[0]
    lats = latitude_factors.shape[1]
    tiles = lats // LANES
    group = fields // n_ord
    pieces = group // FIELDS
    chunks = pieces * orders // CHUNK
    total = n_ord * orders
    spans = n_ord // 2
    early = pieces > 1
    height = n_ord * ROWS
    hbm_spec = pl.BlockSpec(memory_space=pltpu.HBM)
    vmem_spec = pl.BlockSpec(memory_space=pltpu.VMEM)
    dma = pltpu.SemaphoreType.DMA
    bf16 = jnp.bfloat16
    out_shape = [
        pltpu.VMEM((pieces, total, ROWS, rank), bf16),
        pltpu.VMEM((tiles, total, LANES, rank), bf16),
        pltpu.VMEM((2, QUAD * NLON, 8 * total), bf16),
    ]
    if early:
        out_shape += [
            pltpu.VMEM((pieces // 2, NLON, 16, lats), bf16),
            pltpu.VMEM((NLON, 8, lats), bf16),
        ]
    coefficients = coefficients.reshape(orders, parts, n_ord, group, depth)
    hold = functools.partial(pltpu.with_memory_space_constraint, memory_space=pltpu.HBM)
    return pl.pallas_call(
        functools.partial(butterfly_kernel, n_ord, n_blk, early),
        out_shape=tuple(out_shape),
        in_specs=[hbm_spec] * 5,
        out_specs=tuple([vmem_spec] * len(out_shape)),
        scratch_shapes=[
            pltpu.VMEM((pieces, orders, n_ord, parts, FIELDS, depth), bf16),
            pltpu.VMEM(leaf_factors.shape, bf16),
            pltpu.VMEM(interpolants.shape, bf16),
            pltpu.VMEM((1, total), jnp.int32),
            pltpu.VMEM((levels, chunks, CHUNK, height, rank), bf16),
            pltpu.VMEM((chunks, n_ord, CHUNK, ROWS, rank), bf16),
            pltpu.VMEM((levels, chunks, CHUNK, height, rank), bf16),
            pltpu.VMEM((2, 8 * total, 2 * LANES), bf16),
            pltpu.VMEM((QUAD * NLON, LANES), jnp.float32),
            dma((pieces, orders, parts)),
            dma((orders,)),
            dma,
            dma,
            dma((tiles,)),
            dma((levels, chunks)),
            dma((levels, chunks)),
            dma((chunks, n_ord)),
            dma((chunks, n_ord)),
            dma((chunks,)),
            dma((spans, tiles)),
            dma((2 * spans, tiles)),
            dma((spans, tiles)),
        ],
        compiler_params=pltpu.CompilerParams(
            collective_id=0, has_side_effects=True, vmem_limit_bytes=24 * MIB
        ),
        name="butterfly",
    )(
        hold(coefficients), hold(leaf_factors), hold(interpolants), hold(latitude_factors),
        hold(order_ids[None, :]),
    )


def products_kernel(early, rows, lat, wide, *refs):
    if early:
        done, half, out, values, first, stage, done_sem, stage_sem = refs
    else:
        out, values, first, stage, stage_sem = refs
    pieces = rows.shape[0]
    tiles = lat.shape[0]
    deep = stage.shape[2]
    pairs = out.shape[1]
    whole = pairs // deep - 1

    def done_out(h):
        return pltpu.make_async_copy(
            done.at[h], out.at[:, pl.ds(h * deep, deep)], done_sem.at[h]
        )

    def stage_out(t):
        lanes = pl.ds(pl.multiple_of(t * LANES, LANES), LANES)
        return pltpu.make_async_copy(
            stage.at[t], out.at[:, pl.ds(whole * deep, deep), lanes], stage_sem.at[t]
        )

    for h in range(whole):
        done_out(h).start()

    @pl.loop(0, tiles)
    def _(t):
        lanes = pl.ds(pl.multiple_of(t * LANES, LANES), LANES)

        def store(at, count, mixed):
            where = pl.ds(at, count)
            if early:
                mixed = jnp.concatenate([half[where, :, lanes], mixed], axis=1)
            stage[t, where] = mixed

        products_unit(rows, lat, wide, values, first, pieces - 1, t, store)
        stage_out(t).start()

    for h in range(whole):
        done_out(h).wait()
    for t in range(tiles):
        stage_out(t).wait()


def products_of(rows, lat, wide, *more):
    pieces, total, _, rank = rows.shape
    tiles = lat.shape[0]
    early = len(more) > 0
    pairs = pieces * FIELDS // 2
    deep = 16 if early else 8
    dma = pltpu.SemaphoreType.DMA
    scratch = [
        pltpu.VMEM((2, 8 * total, 2 * LANES), jnp.bfloat16),
        pltpu.VMEM((QUAD * NLON, LANES), jnp.float32),
        pltpu.VMEM((tiles, NLON, deep, LANES), jnp.bfloat16),
    ]
    if early:
        scratch.append(dma((max(pairs // deep - 1, 1),)))
    scratch.append(dma((tiles,)))
    operands = [
        pltpu.with_memory_space_constraint(x, memory_space=pltpu.VMEM)
        for x in (rows, lat, wide, *more)
    ]
    return pl.pallas_call(
        functools.partial(products_kernel, early),
        out_shape=jax.ShapeDtypeStruct((NLON, pairs, tiles * LANES), jnp.bfloat16),
        in_specs=[pl.BlockSpec(memory_space=pltpu.VMEM)] * len(operands),
        out_specs=pl.BlockSpec(memory_space=pl.ANY),
        scratch_shapes=scratch,
        compiler_params=pltpu.CompilerParams(vmem_limit_bytes=12 * MIB),
        name="products",
    )(*operands)


def per_device(coefficients, leaf_factors, level_interpolants, latitude_factors, order_ids):
    return products_of(
        *butterfly(
            coefficients, leaf_factors, level_interpolants, latitude_factors, order_ids,
            lax.axis_size("ord"), lax.axis_size("blk"),
        )
    )


def solution(mesh):
    in_specs = (
        P("ord", None, None, "blk"),
        P("ord", None, "blk"),
        P(None, None, "ord", None, "blk"),
        P("ord", "blk", None),
        P(),
    )
    out_specs = P(None, "ord", "blk")
    return jax.shard_map(
        per_device, mesh=mesh, in_specs=in_specs, out_specs=out_specs, check_vma=False
    )
```

```python
import functools
import math

import jax
import jax.numpy as jnp
from jax import lax
from jax.experimental import pallas as pl
from jax.experimental.pallas import tpu as pltpu
from jax.sharding import PartitionSpec as P

PERIOD = 16384
NLON = 256
LANES = 128
FIELDS = 16
ROWS = 2 * FIELDS
QUAD = 4
CHUNK = 2
WINDOW = 2
LEVEL_LAG = 2
FIRST_UNIT = 23
UNIT_DELAY = 12
LAT_STEP = 2
LAT_PASS = 4
MIB = 2**20
MESH = pl.DeviceIdType.MESH
NT = (((1,), (1,)), ((), ()))


def iota(shape, dimension):
    return lax.broadcasted_iota(jnp.int32, shape, dimension)


def synthesis_table(order_ids, count, period):
    steps = iota((count, order_ids.shape[1]), 0)
    phase = lax.rem(steps * order_ids, period).astype(jnp.float32) * (2.0 * math.pi / period)
    weight = jnp.where(order_ids == 0, 1.0, 2.0).astype(jnp.float32)
    table = jnp.concatenate([weight * jnp.cos(phase), -weight * jnp.sin(phase)], axis=1)
    return table.astype(jnp.bfloat16)


def spread_tables(order_ids, wide_ref):
    total = order_ids.shape[1]
    table = synthesis_table(order_ids, NLON, PERIOD)
    tall, broad = wide_ref.shape[1:]
    row, column = iota((2 * total, broad), 0), iota((2 * total, broad), 1)
    source = ((column >> 2) & 1) * total + (column >> 3)
    columns = (row == source).astype(jnp.float32).astype(jnp.bfloat16)
    step = min(tall, 256)
    for side in range(2):
        for r in range(0, tall, step):
            row, lon = iota((step, NLON), 0) + r, iota((step, NLON), 1)
            rows = (((row >> 2) ^ side) == lon).astype(jnp.float32).astype(jnp.bfloat16)
            some = jnp.dot(rows, table, preferred_element_type=jnp.float32).astype(jnp.bfloat16)
            most = jnp.dot(some, columns, preferred_element_type=jnp.float32)
            keep = (iota((step, broad), 0) & 3) == (iota((step, broad), 1) & 3)
            wide_ref[side, pl.ds(r, step), :] = jnp.where(keep, most, 0.0).astype(jnp.bfloat16)


def row_order():
    size = 128
    to, come = iota((size, size), 0), iota((size, size), 1)
    inside = to & 31
    block, parity, part, pair = inside >> 4, (inside >> 3) & 1, (inside >> 2) & 1, inside & 3
    source = (to - inside) + part * FIELDS + block * 8 + pair * 2 + parity
    return (source == come).astype(jnp.float32).astype(jnp.bfloat16)


def map_rows(rows, lat, views, f, tiles, m):
    nil = jnp.zeros((ROWS, rows.shape[3]), jnp.bfloat16)
    both = jnp.concatenate(
        [
            jnp.concatenate([rows[f, 2 * m], nil], axis=1),
            jnp.concatenate([nil, rows[f, 2 * m + 1]], axis=1),
        ],
        axis=0,
    )
    factors = jnp.concatenate(
        [jnp.concatenate([lat[t, 2 * m], lat[t, 2 * m + 1]], axis=1) for t in tiles], axis=0
    )
    mapped = lax.dot_general(both, factors, NT, preferred_element_type=jnp.float32)
    for x, view in enumerate(views):
        part = mapped[:, x * LANES : (x + 1) * LANES]
        for q in range(4):
            view[q // 2, 16 * m : 16 * m + 16, (q % 2) * LANES : (q % 2 + 1) * LANES] = (
                jnp.concatenate([part[8 * q : 8 * q + 8], part[ROWS + 8 * q : ROWS + 8 * q + 8]])
            ).astype(jnp.bfloat16)


def multiply_fields(wide, view, first, block, r, store):
    step = 256
    grid = jnp.dot(wide[block, r : r + step], view[block], preferred_element_type=jnp.float32)
    here = grid[:, :LANES] * grid[:, LANES:]
    if block == 0:
        first[r : r + step] = here
        return
    low = iota((step // 8, 8, LANES), 1) < QUAD
    here = here.reshape(step // 8, 8, LANES)
    there = first[r : r + step].reshape(step // 8, 8, LANES)
    even = jnp.where(low, there, here)
    odd = pltpu.roll(jnp.where(low, here, there), QUAD, 1)
    mixed = jnp.concatenate([even[:, None], odd[:, None]], axis=1)
    store(r // QUAD, step // QUAD, mixed.reshape(step // QUAD, 8, LANES).astype(jnp.bfloat16))


def together(main, more):
    given = 0
    for n, step in enumerate(main):
        until = (n + 1) * len(more) // len(main)
        for other in more[given:until]:
            other()
        given = until
        step()


def multiply_steps(wide, view, first, store):
    return [
        functools.partial(multiply_fields, wide, view, first, block, r, store)
        for block in range(2)
        for r in range(0, wide.shape[1], 256)
    ]


def map_steps(rows, lat, views, f, tiles):
    return [
        functools.partial(map_rows, rows, lat, views, f, tiles, m)
        for m in range(rows.shape[1] // 2)
    ]


def butterfly_kernel(
    n_ord, n_blk, early, coef_hbm, leaf_hbm, interp_hbm, lat_hbm, ids_hbm, *refs,
):
    if early:
        rows, lat, wide, done, half, *refs = refs
    else:
        rows, lat, wide, *refs = refs
    (
        coef, leaf, interp, ids, own, last, came, values, first,
        coef_sem, piece_sem, leaf_sem, interp_sem, ids_sem, lat_in_sem,
        level_send, level_recv, group_send, group_recv, own_sem,
        lat_send, lat_recv, lat_pass,
    ) = refs
    me_ord, me_blk = lax.axis_index("ord"), lax.axis_index("blk")
    pieces, orders, _, parts, _, depth = coef.shape
    levels = interp.shape[0]
    per_piece = orders // CHUNK
    chunks = pieces * per_piece
    tiles = lat.shape[0]
    height = n_ord * ROWS
    rank = interp.shape[-1]
    steps = chunks + LEVEL_LAG * (levels - 1)

    def coef_in(f, i, part):
        return pltpu.make_async_copy(
            coef_hbm.at[i, part, :, pl.ds(pl.multiple_of(f * FIELDS, FIELDS), FIELDS)],
            coef.at[f, i, :, part], coef_sem.at[i, part],
        )

    def piece_in(f, part):
        return pltpu.make_async_copy(
            coef_hbm.at[:, part, :, pl.ds(pl.multiple_of(f * FIELDS, FIELDS), FIELDS)],
            coef.at[f, :, :, part], piece_sem.at[f, part],
        )

    def leaf_in(i):
        return pltpu.make_async_copy(leaf_hbm.at[i], leaf.at[i], leaf_sem.at[i])

    interp_in = pltpu.make_async_copy(interp_hbm, interp, interp_sem)
    ids_in = pltpu.make_async_copy(ids_hbm, ids, ids_sem)

    def lat_rows(t, o):
        return lat.at[t, pl.ds(pl.multiple_of(o * orders, orders), orders)]

    def lat_in(t):
        return pltpu.make_async_copy(
            lat_hbm.at[:, pl.ds(t * LANES, LANES)], lat_rows(t, me_ord), lat_in_sem.at[t]
        )

    barrier = pltpu.get_barrier_semaphore()
    partners = [me_blk ^ (n_blk >> (k + 1)) for k in range(levels)]
    for k in range(levels):
        pl.semaphore_signal(barrier, inc=1, device_id={"blk": partners[k]}, device_id_type=MESH)
    for d in range(1, n_ord):
        pl.semaphore_signal(
            barrier, inc=1, device_id={"ord": lax.rem(me_ord + d, n_ord)}, device_id_type=MESH
        )

    def load_orders(begin, end):
        for i in range(begin, end):
            leaf_in(i).start()
            for part in range(parts):
                coef_in(0, i, part).start()

    load_orders(0, 2 * CHUNK)
    for t in range(tiles):
        lat_in(t).start()
    interp_in.start()

    def leaf_step(c):
        f, i = c // per_piece, lax.rem(c, per_piece) * CHUNK

        @pl.when(f == 0)
        def _():
            for h in range(CHUNK):
                leaf_in(i + h).wait()
                for part in range(parts):
                    coef_in(0, i + h, part).wait()

        @pl.when((f > 0) & (i == 0))
        def _():
            for part in range(parts):
                piece_in(f, part).wait()

        order = row_order()
        for h in range(CHUNK):
            reduced = lax.dot_general(
                coef[f, i + h].reshape(height, depth), leaf[i + h], NT,
                preferred_element_type=jnp.float32,
            ).astype(jnp.bfloat16)
            for r in range(0, height, 128):
                own[0, c, h, r : r + 128] = jnp.dot(
                    order, reduced[r : r + 128], preferred_element_type=jnp.float32
                ).astype(jnp.bfloat16)

    leaf_step(0)
    pl.semaphore_wait(barrier, levels + n_ord - 1)

    def level_copy(k, c):
        return pltpu.make_async_remote_copy(
            src_ref=own.at[k, c], dst_ref=came.at[k, c],
            send_sem=level_send.at[k, c], recv_sem=level_recv.at[k, c],
            device_id={"blk": partners[k]}, device_id_type=MESH,
        )

    def landing(c):
        at = me_ord * orders + lax.rem(c, per_piece) * CHUNK
        return rows.at[c // per_piece, pl.ds(at, CHUNK)]

    def group_copy(c, d):
        peer = lax.rem(me_ord + d, n_ord)
        return pltpu.make_async_remote_copy(
            src_ref=last.at[c, peer], dst_ref=landing(c),
            send_sem=group_send.at[c, d], recv_sem=group_recv.at[c, d],
            device_id={"ord": peer}, device_id_type=MESH,
        )

    def own_copy(c):
        return pltpu.make_async_copy(last.at[c, me_ord], landing(c), own_sem.at[c])

    spans = n_ord // 2
    mate = me_ord ^ 1

    def lat_copy(d, t):
        target = mate if d == 0 else lax.rem(me_ord + 2 * d, n_ord)
        return pltpu.make_async_remote_copy(
            src_ref=lat_rows(t, me_ord), dst_ref=lat_rows(t, me_ord),
            send_sem=lat_send.at[d, t], recv_sem=lat_recv.at[d, t],
            device_id={"ord": target}, device_id_type=MESH,
        )

    def lat_forward(d, t):
        source = lax.rem(me_ord + n_ord - 2 * d, n_ord)
        return pltpu.make_async_remote_copy(
            src_ref=lat_rows(t, source), dst_ref=lat_rows(t, source),
            send_sem=lat_pass.at[d, t], recv_sem=lat_recv.at[spans + d, t],
            device_id={"ord": mate}, device_id_type=MESH,
        )

    def lat_start(t):
        lat_in(t).wait()
        for d in range(spans - 1, -1, -1):
            lat_copy(d, t).start()

    def lat_pass_on(t):
        for d in range(1, spans):
            lat_copy(d, t).wait_recv()
            lat_forward(d, t).start()

    def lat_arrived(t):
        lat_copy(0, t).wait_recv()
        for d in range(1, spans):
            lat_forward(d, t).wait_recv()

    def rows_arrived(f):
        for n in range(per_piece):
            for d in range(1, n_ord):
                group_copy(f * per_piece + n, d).wait_recv()
            own_copy(f * per_piece + n).wait()

    level_copy(0, 0).start()
    load_orders(2 * CHUNK, orders)

    for c in range(1, WINDOW):
        leaf_step(c)
        level_copy(0, c).start()

    for f in range(1, pieces):
        for part in range(parts):
            piece_in(f, part).start()
    ids_in.start()
    for t in range(tiles):
        lat_start(t)
    interp_in.wait()

    def level_step(k, s):
        c = s - k * LEVEL_LAG

        @pl.when((c >= 0) & (c < chunks))
        def _():
            i = lax.rem(c, per_piece) * CHUNK
            level_copy(k, c).wait_recv()
            if k == 0:
                @pl.when(s + WINDOW < chunks)
                def _():
                    level_copy(0, s + WINDOW).start()

            for h in range(CHUNK):
                both = jnp.concatenate([own[k, c, h], came[k, c, h]], axis=1)
                factors = jnp.concatenate([interp[k, 0, i + h], interp[k, 1, i + h]], axis=1)
                mixed = lax.dot_general(
                    both, factors, NT, preferred_element_type=jnp.float32
                ).astype(jnp.bfloat16)
                if k + 1 < levels:
                    own[k + 1, c, h] = mixed
                else:
                    last[c, :, h] = mixed.reshape(n_ord, ROWS, rank)
            if k + 1 < levels:
                level_copy(k + 1, c).start()
            else:
                for d in range(1, n_ord):
                    group_copy(c, d).start()
                own_copy(c).start()

    begins = []
    for f in range(pieces - 1):
        begins.append(max(FIRST_UNIT + f * (tiles + 1), 2 * (f * per_piece + UNIT_DELAY - 2)))

    @pl.loop(0, max([2 * steps] + [b + tiles + 1 for b in begins]))
    def _(j):
        s = j // 2

        @pl.when(lax.rem(j, 2) == 0)
        def _():
            @pl.when(s + WINDOW < chunks)
            def _():
                leaf_step(s + WINDOW)

            level_step(0, s)

            @pl.when(s == 2)
            def _():
                ids_in.wait()
                spread_tables(ids[...], wide)
                if early:
                    half[...] = jnp.zeros(half.shape, half.dtype)

            for t in range(tiles):
                @pl.when(s == min(LAT_STEP * t + LAT_PASS, steps - 1))
                def _():
                    lat_pass_on(t)

        @pl.when(lax.rem(j, 2) == 1)
        def _():
            for k in range(1, levels):
                level_step(k, s)

        if early:
            f = sum((j >= b).astype(jnp.int32) for b in begins) - 1
            begin = begins[0]
            for before, b in zip(begins, begins[1:]):
                begin = begin + (j >= b).astype(jnp.int32) * (b - before)
            v = j - begin

            @pl.when((f >= 0) & (v <= tiles))
            def _():
                @pl.when((f == 0) & (v < tiles))
                def _():
                    lat_arrived(v)

                lanes = pl.ds(pl.multiple_of((v - 1) * LANES, LANES), LANES)

                def store(at, count, mixed):
                    where = pl.ds(at, count)
                    done[f // 2, where, :, lanes] = jnp.concatenate(
                        [half[where, :, lanes], mixed], axis=1
                    )
                    half[where, :, lanes] = mixed

                new, old = values.at[lax.rem(v, 2)], values.at[lax.rem(v + 1, 2)]

                @pl.when(v == 0)
                def _():
                    rows_arrived(f)
                    for step in map_steps(rows, lat, [new], f, [v]):
                        step()

                @pl.when((v > 0) & (v < tiles))
                def _():
                    together(
                        multiply_steps(wide, old, first, store),
                        map_steps(rows, lat, [new], f, [v]),
                    )

                @pl.when(v == tiles)
                def _():
                    for step in multiply_steps(wide, old, first, store):
                        step()

    if not early:
        for t in range(tiles):
            lat_arrived(t)
    for f in range(len(begins), pieces):
        rows_arrived(f)

    for t in range(tiles):
        for d in range(spans):
            lat_copy(d, t).wait_send()
        for d in range(1, spans):
            lat_forward(d, t).wait_send()

    @pl.loop(0, chunks)
    def _(c):
        for k in range(levels):
            level_copy(k, c).wait_send()
        for d in range(1, n_ord):
            group_copy(c, d).wait_send()


def butterfly(coefficients, leaf_factors, interpolants, latitude_factors, order_ids, n_ord, n_blk):
    orders, parts, fields, depth = coefficients.shape
    rank = leaf_factors.shape[1]
    levels = interpolants.shape[0]
    lats = latitude_factors.shape[1]
    tiles = lats // LANES
    group = fields // n_ord
    pieces = group // FIELDS
    chunks = pieces * orders // CHUNK
    total = n_ord * orders
    spans = n_ord // 2
    early = pieces > 1
    height = n_ord * ROWS
    hbm_spec = pl.BlockSpec(memory_space=pltpu.HBM)
    vmem_spec = pl.BlockSpec(memory_space=pltpu.VMEM)
    dma = pltpu.SemaphoreType.DMA
    bf16 = jnp.bfloat16
    out_shape = [
        pltpu.VMEM((pieces, total, ROWS, rank), bf16),
        pltpu.VMEM((tiles, total, LANES, rank), bf16),
        pltpu.VMEM((2, QUAD * NLON, 8 * total), bf16),
    ]
    if early:
        out_shape += [
            pltpu.VMEM((pieces // 2, NLON, 16, lats), bf16),
            pltpu.VMEM((NLON, 8, lats), bf16),
        ]
    coefficients = coefficients.reshape(orders, parts, n_ord, group, depth)
    hold = functools.partial(pltpu.with_memory_space_constraint, memory_space=pltpu.HBM)
    return pl.pallas_call(
        functools.partial(butterfly_kernel, n_ord, n_blk, early),
        out_shape=tuple(out_shape),
        in_specs=[hbm_spec] * 5,
        out_specs=tuple([vmem_spec] * len(out_shape)),
        scratch_shapes=[
            pltpu.VMEM((pieces, orders, n_ord, parts, FIELDS, depth), bf16),
            pltpu.VMEM(leaf_factors.shape, bf16),
            pltpu.VMEM(interpolants.shape, bf16),
            pltpu.VMEM((1, total), jnp.int32),
            pltpu.VMEM((levels, chunks, CHUNK, height, rank), bf16),
            pltpu.VMEM((chunks, n_ord, CHUNK, ROWS, rank), bf16),
            pltpu.VMEM((levels, chunks, CHUNK, height, rank), bf16),
            pltpu.VMEM((2, 2, 8 * total, 2 * LANES), bf16),
            pltpu.VMEM((QUAD * NLON, LANES), jnp.float32),
            dma((orders, parts)),
            dma((pieces, parts)),
            dma((orders,)),
            dma,
            dma,
            dma((tiles,)),
            dma((levels, chunks)),
            dma((levels, chunks)),
            dma((chunks, n_ord)),
            dma((chunks, n_ord)),
            dma((chunks,)),
            dma((spans, tiles)),
            dma((2 * spans, tiles)),
            dma((spans, tiles)),
        ],
        compiler_params=pltpu.CompilerParams(
            collective_id=0, has_side_effects=True, vmem_limit_bytes=24 * MIB
        ),
        name="butterfly",
    )(
        hold(coefficients), hold(leaf_factors), hold(interpolants), hold(latitude_factors),
        hold(order_ids[None, :]),
    )


def products_kernel(early, rows, lat, wide, *refs):
    if early:
        done, half, out, values, first, stage, done_sem, stage_sem = refs
    else:
        out, values, first, stage, stage_sem = refs
    pieces = rows.shape[0]
    tiles = lat.shape[0]
    deep = stage.shape[2]
    pairs = out.shape[1]
    whole = pairs // deep - 1

    def done_out(h):
        return pltpu.make_async_copy(
            done.at[h], out.at[:, pl.ds(h * deep, deep)], done_sem.at[h]
        )

    def stage_out(t):
        lanes = pl.ds(t * LANES, LANES)
        return pltpu.make_async_copy(
            stage.at[t], out.at[:, pl.ds(whole * deep, deep), lanes], stage_sem.at[t]
        )

    for h in range(whole):
        done_out(h).start()

    def store_at(t):
        def store(at, count, mixed):
            where = pl.ds(at, count)
            if early:
                mixed = jnp.concatenate(
                    [half[where, :, t * LANES : (t + 1) * LANES], mixed], axis=1
                )
            stage[t, where] = mixed

        return store

    sets = [list(range(t, min(t + 2, tiles))) for t in range(0, tiles, 2)]

    def mapped(n):
        views = [values.at[n % 2, x] for x in range(len(sets[n]))]
        return map_steps(rows, lat, views, pieces - 1, sets[n])

    for step in mapped(0):
        step()
    for n, ts in enumerate(sets):
        more = mapped(n + 1) if n + 1 < len(sets) else []
        for x, t in enumerate(ts):
            begin, end = x * len(more) // len(ts), (x + 1) * len(more) // len(ts)
            together(
                multiply_steps(wide, values.at[n % 2, x], first, store_at(t)), more[begin:end]
            )
            stage_out(t).start()

    for h in range(whole):
        done_out(h).wait()
    for t in range(tiles):
        stage_out(t).wait()


def products_of(rows, lat, wide, *more):
    pieces, total, _, rank = rows.shape
    tiles = lat.shape[0]
    early = len(more) > 0
    pairs = pieces * FIELDS // 2
    deep = 16 if early else 8
    dma = pltpu.SemaphoreType.DMA
    scratch = [
        pltpu.VMEM((2, 2, 2, 8 * total, 2 * LANES), jnp.bfloat16),
        pltpu.VMEM((QUAD * NLON, LANES), jnp.float32),
        pltpu.VMEM((tiles, NLON, deep, LANES), jnp.bfloat16),
    ]
    if early:
        scratch.append(dma((max(pairs // deep - 1, 1),)))
    scratch.append(dma((tiles,)))
    operands = [
        pltpu.with_memory_space_constraint(x, memory_space=pltpu.VMEM)
        for x in (rows, lat, wide, *more)
    ]
    return pl.pallas_call(
        functools.partial(products_kernel, early),
        out_shape=jax.ShapeDtypeStruct((NLON, pairs, tiles * LANES), jnp.bfloat16),
        in_specs=[pl.BlockSpec(memory_space=pltpu.VMEM)] * len(operands),
        out_specs=pl.BlockSpec(memory_space=pl.ANY),
        scratch_shapes=scratch,
        compiler_params=pltpu.CompilerParams(vmem_limit_bytes=14 * MIB),
        name="products",
    )(*operands)


def per_device(coefficients, leaf_factors, level_interpolants, latitude_factors, order_ids):
    return products_of(
        *butterfly(
            coefficients, leaf_factors, level_interpolants, latitude_factors, order_ids,
            lax.axis_size("ord"), lax.axis_size("blk"),
        )
    )


def solution(mesh):
    in_specs = (
        P("ord", None, None, "blk"),
        P("ord", None, "blk"),
        P(None, None, "ord", None, "blk"),
        P("ord", "blk", None),
        P(),
    )
    out_specs = P(None, "ord", "blk")
    return jax.shard_map(
        per_device, mesh=mesh, in_specs=in_specs, out_specs=out_specs, check_vma=False
    )
```

```python
import functools
import math

import jax
import jax.numpy as jnp
from jax import lax
from jax.experimental import pallas as pl
from jax.experimental.pallas import tpu as pltpu
from jax.sharding import PartitionSpec as P

PERIOD = 16384
NLON = 256
LANES = 128
FIELDS = 16
ROWS = 2 * FIELDS
QUAD = 4
CHUNK = 2
WINDOW = 2
LEVEL_LAG = 2
FIRST_UNIT = 22
UNIT_DELAY = 11
LAT_STEP = 2
LAT_PASS = 4
MIB = 2**20
MESH = pl.DeviceIdType.MESH
NT = (((1,), (1,)), ((), ()))


def iota(shape, dimension):
    return lax.broadcasted_iota(jnp.int32, shape, dimension)


def synthesis_table(order_ids, count, period):
    steps = iota((count, order_ids.shape[1]), 0)
    phase = lax.rem(steps * order_ids, period).astype(jnp.float32) * (2.0 * math.pi / period)
    weight = jnp.where(order_ids == 0, 1.0, 2.0).astype(jnp.float32)
    table = jnp.concatenate([weight * jnp.cos(phase), -weight * jnp.sin(phase)], axis=1)
    return table.astype(jnp.bfloat16)


def spread_tables(order_ids, wide_ref):
    total = order_ids.shape[1]
    table = synthesis_table(order_ids, NLON, PERIOD)
    tall, broad = wide_ref.shape[1:]
    row, column = iota((2 * total, broad), 0), iota((2 * total, broad), 1)
    source = ((column >> 2) & 1) * total + (column >> 3)
    columns = (row == source).astype(jnp.float32).astype(jnp.bfloat16)
    step = min(tall, 256)
    for side in range(2):
        for r in range(0, tall, step):
            row, lon = iota((step, NLON), 0) + r, iota((step, NLON), 1)
            rows = (((row >> 2) ^ side) == lon).astype(jnp.float32).astype(jnp.bfloat16)
            some = jnp.dot(rows, table, preferred_element_type=jnp.float32).astype(jnp.bfloat16)
            most = jnp.dot(some, columns, preferred_element_type=jnp.float32)
            keep = (iota((step, broad), 0) & 3) == (iota((step, broad), 1) & 3)
            wide_ref[side, pl.ds(r, step), :] = jnp.where(keep, most, 0.0).astype(jnp.bfloat16)


def row_order():
    size = 128
    to, come = iota((size, size), 0), iota((size, size), 1)
    inside = to & 31
    block, parity, part, pair = inside >> 4, (inside >> 3) & 1, (inside >> 2) & 1, inside & 3
    source = (to - inside) + part * FIELDS + block * 8 + pair * 2 + parity
    return (source == come).astype(jnp.float32).astype(jnp.bfloat16)


def map_rows(rows, lat, views, f, tiles, m):
    nil = jnp.zeros((ROWS, rows.shape[3]), jnp.bfloat16)
    both = jnp.concatenate(
        [
            jnp.concatenate([rows[f, 2 * m], nil], axis=1),
            jnp.concatenate([nil, rows[f, 2 * m + 1]], axis=1),
        ],
        axis=0,
    )
    factors = jnp.concatenate(
        [jnp.concatenate([lat[t, 2 * m], lat[t, 2 * m + 1]], axis=1) for t in tiles], axis=0
    )
    mapped = lax.dot_general(both, factors, NT, preferred_element_type=jnp.float32)
    for x, view in enumerate(views):
        part = mapped[:, x * LANES : (x + 1) * LANES]
        for q in range(4):
            view[q // 2, 16 * m : 16 * m + 16, (q % 2) * LANES : (q % 2 + 1) * LANES] = (
                jnp.concatenate([part[8 * q : 8 * q + 8], part[ROWS + 8 * q : ROWS + 8 * q + 8]])
            ).astype(jnp.bfloat16)


def multiply_fields(wide, weights, first, block, r, store):
    step = 256
    grid = jnp.dot(wide[block, r : r + step], weights(block), preferred_element_type=jnp.float32)
    here = grid[:, :LANES] * grid[:, LANES:]
    if block == 0:
        first[r : r + step] = here
        return
    low = iota((step // 8, 8, LANES), 1) < QUAD
    here = here.reshape(step // 8, 8, LANES)
    there = first[r : r + step].reshape(step // 8, 8, LANES)
    even = jnp.where(low, there, here)
    odd = pltpu.roll(jnp.where(low, here, there), QUAD, 1)
    mixed = jnp.concatenate([even[:, None], odd[:, None]], axis=1)
    store(r // QUAD, step // QUAD, mixed.reshape(step // QUAD, 8, LANES).astype(jnp.bfloat16))


def together(main, more):
    given = 0
    for n, step in enumerate(main):
        until = (n + 1) * len(more) // len(main)
        for other in more[given:until]:
            other()
        given = until
        step()


def multiply_steps(wide, weights, first, store):
    return [
        functools.partial(multiply_fields, wide, weights, first, block, r, store)
        for block in range(2)
        for r in range(0, wide.shape[1], 256)
    ]


def tile_sets(tiles):
    return [list(range(t, min(t + 2, tiles))) for t in range(0, tiles, 2)]


def order_pairs(total, orders, late):
    return [m for m in range(total // 2) if (2 * m % orders >= orders - CHUNK) == late]


def map_steps(rows, lat, views, f, tiles, pairs=None):
    return [
        functools.partial(map_rows, rows, lat, views, f, tiles, m)
        for m in (range(rows.shape[1] // 2) if pairs is None else pairs)
    ]


def butterfly_kernel(
    n_ord, n_blk, early, coef_hbm, leaf_hbm, interp_hbm, lat_hbm, ids_hbm, *refs,
):
    if early:
        rows, lat, wide, ready, done, half, *refs = refs
    else:
        rows, lat, wide, ready, *refs = refs
    (
        coef, leaf, interp, ids, own, last, came, values, first,
        coef_sem, piece_sem, leaf_sem, interp_sem, ids_sem, lat_in_sem,
        level_send, level_recv, group_send, group_recv, own_sem,
        lat_send, lat_recv, lat_pass,
    ) = refs
    me_ord, me_blk = lax.axis_index("ord"), lax.axis_index("blk")
    pieces, orders, _, parts, _, depth = coef.shape
    levels = interp.shape[0]
    per_piece = orders // CHUNK
    chunks = pieces * per_piece
    tiles = lat.shape[0]
    height = n_ord * ROWS
    total = n_ord * orders
    rank = interp.shape[-1]
    steps = chunks + LEVEL_LAG * (levels - 1)

    def coef_in(f, i, part):
        return pltpu.make_async_copy(
            coef_hbm.at[i, part, :, pl.ds(pl.multiple_of(f * FIELDS, FIELDS), FIELDS)],
            coef.at[f, i, :, part], coef_sem.at[i, part],
        )

    def piece_in(f, part):
        return pltpu.make_async_copy(
            coef_hbm.at[:, part, :, pl.ds(pl.multiple_of(f * FIELDS, FIELDS), FIELDS)],
            coef.at[f, :, :, part], piece_sem.at[f, part],
        )

    def leaf_in(i):
        return pltpu.make_async_copy(leaf_hbm.at[i], leaf.at[i], leaf_sem.at[i])

    interp_in = pltpu.make_async_copy(interp_hbm, interp, interp_sem)
    ids_in = pltpu.make_async_copy(ids_hbm, ids, ids_sem)

    def lat_rows(t, o):
        return lat.at[t, pl.ds(pl.multiple_of(o * orders, orders), orders)]

    def lat_in(t):
        return pltpu.make_async_copy(
            lat_hbm.at[:, pl.ds(t * LANES, LANES)], lat_rows(t, me_ord), lat_in_sem.at[t]
        )

    barrier = pltpu.get_barrier_semaphore()
    partners = [me_blk ^ (n_blk >> (k + 1)) for k in range(levels)]
    for k in range(levels):
        pl.semaphore_signal(barrier, inc=1, device_id={"blk": partners[k]}, device_id_type=MESH)
    for d in range(1, n_ord):
        pl.semaphore_signal(
            barrier, inc=1, device_id={"ord": lax.rem(me_ord + d, n_ord)}, device_id_type=MESH
        )

    def load_orders(begin, end):
        for i in range(begin, end):
            leaf_in(i).start()
            for part in range(parts):
                coef_in(0, i, part).start()

    load_orders(0, 2 * CHUNK)
    for t in range(tiles):
        lat_in(t).start()
    interp_in.start()

    def leaf_step(c):
        f, i = c // per_piece, lax.rem(c, per_piece) * CHUNK

        @pl.when(f == 0)
        def _():
            for h in range(CHUNK):
                leaf_in(i + h).wait()
                for part in range(parts):
                    coef_in(0, i + h, part).wait()

        @pl.when((f > 0) & (i == 0))
        def _():
            for part in range(parts):
                piece_in(f, part).wait()

        order = row_order()
        for h in range(CHUNK):
            reduced = lax.dot_general(
                coef[f, i + h].reshape(height, depth), leaf[i + h], NT,
                preferred_element_type=jnp.float32,
            ).astype(jnp.bfloat16)
            for r in range(0, height, 128):
                own[0, c, h, r : r + 128] = jnp.dot(
                    order, reduced[r : r + 128], preferred_element_type=jnp.float32
                ).astype(jnp.bfloat16)

    leaf_step(0)
    pl.semaphore_wait(barrier, levels + n_ord - 1)

    def level_copy(k, c):
        return pltpu.make_async_remote_copy(
            src_ref=own.at[k, c], dst_ref=came.at[k, c],
            send_sem=level_send.at[k, c], recv_sem=level_recv.at[k, c],
            device_id={"blk": partners[k]}, device_id_type=MESH,
        )

    def landing(c):
        at = me_ord * orders + lax.rem(c, per_piece) * CHUNK
        return rows.at[c // per_piece, pl.ds(at, CHUNK)]

    def group_copy(c, d):
        peer = lax.rem(me_ord + d, n_ord)
        return pltpu.make_async_remote_copy(
            src_ref=last.at[c, peer], dst_ref=landing(c),
            send_sem=group_send.at[c, d], recv_sem=group_recv.at[c, d],
            device_id={"ord": peer}, device_id_type=MESH,
        )

    def own_copy(c):
        return pltpu.make_async_copy(last.at[c, me_ord], landing(c), own_sem.at[c])

    spans = n_ord // 2
    mate = me_ord ^ 1

    def lat_copy(d, t):
        target = mate if d == 0 else lax.rem(me_ord + 2 * d, n_ord)
        return pltpu.make_async_remote_copy(
            src_ref=lat_rows(t, me_ord), dst_ref=lat_rows(t, me_ord),
            send_sem=lat_send.at[d, t], recv_sem=lat_recv.at[d, t],
            device_id={"ord": target}, device_id_type=MESH,
        )

    def lat_forward(d, t):
        source = lax.rem(me_ord + n_ord - 2 * d, n_ord)
        return pltpu.make_async_remote_copy(
            src_ref=lat_rows(t, source), dst_ref=lat_rows(t, source),
            send_sem=lat_pass.at[d, t], recv_sem=lat_recv.at[spans + d, t],
            device_id={"ord": mate}, device_id_type=MESH,
        )

    def lat_start(t):
        lat_in(t).wait()
        for d in range(spans - 1, -1, -1):
            lat_copy(d, t).start()

    def lat_pass_on(t):
        for d in range(1, spans):
            lat_copy(d, t).wait_recv()
            lat_forward(d, t).start()

    def lat_arrived(t):
        lat_copy(0, t).wait_recv()
        for d in range(1, spans):
            lat_forward(d, t).wait_recv()

    def rows_arrived(f, begin, end):
        for n in range(begin, end):
            for d in range(1, n_ord):
                group_copy(f * per_piece + n, d).wait_recv()
            own_copy(f * per_piece + n).wait()

    level_copy(0, 0).start()
    load_orders(2 * CHUNK, orders)

    for c in range(1, WINDOW):
        leaf_step(c)
        level_copy(0, c).start()

    for f in range(1, pieces):
        for part in range(parts):
            piece_in(f, part).start()
    ids_in.start()
    for t in range(tiles):
        lat_start(t)
    interp_in.wait()

    def level_step(k, s):
        c = s - k * LEVEL_LAG

        @pl.when((c >= 0) & (c < chunks))
        def _():
            i = lax.rem(c, per_piece) * CHUNK
            level_copy(k, c).wait_recv()
            if k == 0:
                @pl.when(s + WINDOW < chunks)
                def _():
                    level_copy(0, s + WINDOW).start()

            for h in range(CHUNK):
                both = jnp.concatenate([own[k, c, h], came[k, c, h]], axis=1)
                factors = jnp.concatenate([interp[k, 0, i + h], interp[k, 1, i + h]], axis=1)
                mixed = lax.dot_general(
                    both, factors, NT, preferred_element_type=jnp.float32
                ).astype(jnp.bfloat16)
                if k + 1 < levels:
                    own[k + 1, c, h] = mixed
                else:
                    last[c, :, h] = mixed.reshape(n_ord, ROWS, rank)
            if k + 1 < levels:
                level_copy(k + 1, c).start()
            else:
                for d in range(1, n_ord):
                    group_copy(c, d).start()
                own_copy(c).start()

    begins = []
    for f in range(pieces - 1):
        begins.append(max(FIRST_UNIT + f * (tiles + 1), 2 * (f * per_piece + UNIT_DELAY - 2)))

    @pl.loop(0, max([2 * steps] + [b + tiles + 1 for b in begins]))
    def _(j):
        s = j // 2

        @pl.when(lax.rem(j, 2) == 0)
        def _():
            @pl.when(s + WINDOW < chunks)
            def _():
                leaf_step(s + WINDOW)

            level_step(0, s)

            @pl.when(s == 2)
            def _():
                ids_in.wait()
                spread_tables(ids[...], wide)
                if early:
                    half[...] = jnp.zeros(half.shape, half.dtype)

            for t in range(tiles):
                @pl.when(s == min(LAT_STEP * t + LAT_PASS, steps - 1))
                def _():
                    lat_pass_on(t)

        @pl.when(lax.rem(j, 2) == 1)
        def _():
            for k in range(1, levels):
                level_step(k, s)

        if early:
            f = sum((j >= b).astype(jnp.int32) for b in begins) - 1
            begin = begins[0]
            for before, b in zip(begins, begins[1:]):
                begin = begin + (j >= b).astype(jnp.int32) * (b - before)
            v = j - begin

            @pl.when((f >= 0) & (v <= tiles))
            def _():
                @pl.when((f == 0) & (v < tiles))
                def _():
                    lat_arrived(v)

                lanes = pl.ds(pl.multiple_of((v - 1) * LANES, LANES), LANES)

                def store(at, count, mixed):
                    where = pl.ds(at, count)
                    done[f // 2, where, :, lanes] = jnp.concatenate(
                        [half[where, :, lanes], mixed], axis=1
                    )
                    half[where, :, lanes] = mixed

                new, was = values.at[lax.rem(v, 2)], values.at[lax.rem(v + 1, 2)]

                def old(block):
                    return was[block]

                @pl.when(v == 0)
                def _():
                    rows_arrived(f, 0, per_piece)
                    for step in map_steps(rows, lat, [new], f, [v]):
                        step()

                @pl.when((v > 0) & (v < tiles))
                def _():
                    together(
                        multiply_steps(wide, old, first, store),
                        map_steps(rows, lat, [new], f, [v]),
                    )

                @pl.when(v == tiles)
                def _():
                    for step in multiply_steps(wide, old, first, store):
                        step()

    if not early:
        for t in range(tiles):
            lat_arrived(t)
    rows_arrived(pieces - 1, 0, per_piece - 1)
    for ts in tile_sets(tiles):
        views = [ready.at[t] for t in ts]
        for step in map_steps(rows, lat, views, pieces - 1, ts, order_pairs(total, orders, False)):
            step()
    rows_arrived(pieces - 1, per_piece - 1, per_piece)

    for t in range(tiles):
        for d in range(spans):
            lat_copy(d, t).wait_send()
        for d in range(1, spans):
            lat_forward(d, t).wait_send()

    @pl.loop(0, chunks)
    def _(c):
        for k in range(levels):
            level_copy(k, c).wait_send()
        for d in range(1, n_ord):
            group_copy(c, d).wait_send()


def butterfly(coefficients, leaf_factors, interpolants, latitude_factors, order_ids, n_ord, n_blk):
    orders, parts, fields, depth = coefficients.shape
    rank = leaf_factors.shape[1]
    levels = interpolants.shape[0]
    lats = latitude_factors.shape[1]
    tiles = lats // LANES
    group = fields // n_ord
    pieces = group // FIELDS
    chunks = pieces * orders // CHUNK
    total = n_ord * orders
    spans = n_ord // 2
    early = pieces > 1
    height = n_ord * ROWS
    hbm_spec = pl.BlockSpec(memory_space=pltpu.HBM)
    vmem_spec = pl.BlockSpec(memory_space=pltpu.VMEM)
    dma = pltpu.SemaphoreType.DMA
    bf16 = jnp.bfloat16
    out_shape = [
        pltpu.VMEM((pieces, total, ROWS, rank), bf16),
        pltpu.VMEM((tiles, total, LANES, rank), bf16),
        pltpu.VMEM((2, QUAD * NLON, 8 * total), bf16),
        pltpu.VMEM((tiles, 2, 8 * total, 2 * LANES), bf16),
    ]
    if early:
        out_shape += [
            pltpu.VMEM((pieces // 2, NLON, 16, lats), bf16),
            pltpu.VMEM((NLON, 8, lats), bf16),
        ]
    coefficients = coefficients.reshape(orders, parts, n_ord, group, depth)
    hold = functools.partial(pltpu.with_memory_space_constraint, memory_space=pltpu.HBM)
    return pl.pallas_call(
        functools.partial(butterfly_kernel, n_ord, n_blk, early),
        out_shape=tuple(out_shape),
        in_specs=[hbm_spec] * 5,
        out_specs=tuple([vmem_spec] * len(out_shape)),
        scratch_shapes=[
            pltpu.VMEM((pieces, orders, n_ord, parts, FIELDS, depth), bf16),
            pltpu.VMEM(leaf_factors.shape, bf16),
            pltpu.VMEM(interpolants.shape, bf16),
            pltpu.VMEM((1, total), jnp.int32),
            pltpu.VMEM((levels, chunks, CHUNK, height, rank), bf16),
            pltpu.VMEM((chunks, n_ord, CHUNK, ROWS, rank), bf16),
            pltpu.VMEM((levels, chunks, CHUNK, height, rank), bf16),
            pltpu.VMEM((2, 2, 8 * total, 2 * LANES), bf16),
            pltpu.VMEM((QUAD * NLON, LANES), jnp.float32),
            dma((orders, parts)),
            dma((pieces, parts)),
            dma((orders,)),
            dma,
            dma,
            dma((tiles,)),
            dma((levels, chunks)),
            dma((levels, chunks)),
            dma((chunks, n_ord)),
            dma((chunks, n_ord)),
            dma((chunks,)),
            dma((spans, tiles)),
            dma((2 * spans, tiles)),
            dma((spans, tiles)),
        ],
        compiler_params=pltpu.CompilerParams(
            collective_id=0, has_side_effects=True, vmem_limit_bytes=24 * MIB
        ),
        name="butterfly",
    )(
        hold(coefficients), hold(leaf_factors), hold(interpolants), hold(latitude_factors),
        hold(order_ids[None, :]),
    )


def products_kernel(early, orders, rows, lat, wide, ready, *refs):
    if early:
        done, half, out, values, first, stage, done_sem, stage_sem = refs
    else:
        out, values, first, stage, stage_sem = refs
    pieces = rows.shape[0]
    tiles = lat.shape[0]
    deep = stage.shape[2]
    pairs = out.shape[1]
    whole = pairs // deep - 1

    def done_out(h):
        return pltpu.make_async_copy(
            done.at[h], out.at[:, pl.ds(h * deep, deep)], done_sem.at[h]
        )

    def stage_out(t):
        lanes = pl.ds(t * LANES, LANES)
        return pltpu.make_async_copy(
            stage.at[t], out.at[:, pl.ds(whole * deep, deep), lanes], stage_sem.at[t]
        )

    for h in range(whole):
        done_out(h).start()

    def store_at(t):
        def store(at, count, mixed):
            where = pl.ds(at, count)
            if early:
                mixed = jnp.concatenate(
                    [half[where, :, t * LANES : (t + 1) * LANES], mixed], axis=1
                )
            stage[t, where] = mixed

        return store

    late = order_pairs(rows.shape[1], orders, True)

    def weights_of(t):
        def weights(block):
            pieces_of = []
            for m in range(rows.shape[1] // 2):
                source = values if m in late else ready
                pieces_of.append(source[t, block, 16 * m : 16 * m + 16])
            return jnp.concatenate(pieces_of, axis=0)

        return weights

    sets = tile_sets(tiles)

    def mapped(n):
        views = [values.at[t] for t in sets[n]]
        return map_steps(rows, lat, views, pieces - 1, sets[n], late)

    for step in mapped(0):
        step()
    for n, ts in enumerate(sets):
        more = mapped(n + 1) if n + 1 < len(sets) else []
        for x, t in enumerate(ts):
            begin, end = x * len(more) // len(ts), (x + 1) * len(more) // len(ts)
            together(multiply_steps(wide, weights_of(t), first, store_at(t)), more[begin:end])
            stage_out(t).start()

    for h in range(whole):
        done_out(h).wait()
    for t in range(tiles):
        stage_out(t).wait()


def products_of(orders, rows, lat, wide, ready, *more):
    pieces, total, _, rank = rows.shape
    tiles = lat.shape[0]
    early = len(more) > 0
    pairs = pieces * FIELDS // 2
    deep = 16 if early else 8
    dma = pltpu.SemaphoreType.DMA
    scratch = [
        pltpu.VMEM((tiles, 2, 8 * total, 2 * LANES), jnp.bfloat16),
        pltpu.VMEM((QUAD * NLON, LANES), jnp.float32),
        pltpu.VMEM((tiles, NLON, deep, LANES), jnp.bfloat16),
    ]
    if early:
        scratch.append(dma((max(pairs // deep - 1, 1),)))
    scratch.append(dma((tiles,)))
    operands = [
        pltpu.with_memory_space_constraint(x, memory_space=pltpu.VMEM)
        for x in (rows, lat, wide, ready, *more)
    ]
    return pl.pallas_call(
        functools.partial(products_kernel, early, orders),
        out_shape=jax.ShapeDtypeStruct((NLON, pairs, tiles * LANES), jnp.bfloat16),
        in_specs=[pl.BlockSpec(memory_space=pltpu.VMEM)] * len(operands),
        out_specs=pl.BlockSpec(memory_space=pl.ANY),
        scratch_shapes=scratch,
        compiler_params=pltpu.CompilerParams(vmem_limit_bytes=14 * MIB),
        name="products",
    )(*operands)


def per_device(coefficients, leaf_factors, level_interpolants, latitude_factors, order_ids):
    return products_of(
        coefficients.shape[0],
        *butterfly(
            coefficients, leaf_factors, level_interpolants, latitude_factors, order_ids,
            lax.axis_size("ord"), lax.axis_size("blk"),
        )
    )


def solution(mesh):
    in_specs = (
        P("ord", None, None, "blk"),
        P("ord", None, "blk"),
        P(None, None, "ord", None, "blk"),
        P("ord", "blk", None),
        P(),
    )
    out_specs = P(None, "ord", "blk")
    return jax.shard_map(
        per_device, mesh=mesh, in_specs=in_specs, out_specs=out_specs, check_vma=False
    )
```

```python
import functools
import math

import jax
import jax.numpy as jnp
from jax import lax
from jax.experimental import pallas as pl
from jax.experimental.pallas import tpu as pltpu
from jax.sharding import PartitionSpec as P

PERIOD = 16384
NLON = 256
LANES = 128
FIELDS = 16
ROWS = 2 * FIELDS
QUAD = 4
CHUNK = 2
WINDOW = 2
LEVEL_LAG = 2
FIRST_UNIT = 22
UNIT_DELAY = 11
LAT_STEP = 2
LAT_PASS = 4
MIB = 2**20
MESH = pl.DeviceIdType.MESH
NT = (((1,), (1,)), ((), ()))


def iota(shape, dimension):
    return lax.broadcasted_iota(jnp.int32, shape, dimension)


def synthesis_table(order_ids, count, period):
    steps = iota((count, order_ids.shape[1]), 0)
    phase = lax.rem(steps * order_ids, period).astype(jnp.float32) * (2.0 * math.pi / period)
    weight = jnp.where(order_ids == 0, 1.0, 2.0).astype(jnp.float32)
    table = jnp.concatenate([weight * jnp.cos(phase), -weight * jnp.sin(phase)], axis=1)
    return table.astype(jnp.bfloat16)


def spread_tables(order_ids, wide_ref):
    total = order_ids.shape[1]
    table = synthesis_table(order_ids, NLON, PERIOD)
    tall, broad = wide_ref.shape[1:]
    row, column = iota((2 * total, broad), 0), iota((2 * total, broad), 1)
    source = ((column >> 2) & 1) * total + (column >> 3)
    columns = (row == source).astype(jnp.float32).astype(jnp.bfloat16)
    step = min(tall, 256)
    for side in range(2):
        for r in range(0, tall, step):
            row, lon = iota((step, NLON), 0) + r, iota((step, NLON), 1)
            rows = (((row >> 2) ^ side) == lon).astype(jnp.float32).astype(jnp.bfloat16)
            some = jnp.dot(rows, table, preferred_element_type=jnp.float32).astype(jnp.bfloat16)
            most = jnp.dot(some, columns, preferred_element_type=jnp.float32)
            keep = (iota((step, broad), 0) & 3) == (iota((step, broad), 1) & 3)
            wide_ref[side, pl.ds(r, step), :] = jnp.where(keep, most, 0.0).astype(jnp.bfloat16)


def row_order():
    size = 128
    to, come = iota((size, size), 0), iota((size, size), 1)
    inside = to & 31
    block, parity, part, pair = inside >> 4, (inside >> 3) & 1, (inside >> 2) & 1, inside & 3
    source = (to - inside) + part * FIELDS + block * 8 + pair * 2 + parity
    return (source == come).astype(jnp.float32).astype(jnp.bfloat16)


def map_rows(rows, lat, views, f, tiles, m):
    nil = jnp.zeros((ROWS, rows.shape[3]), jnp.bfloat16)
    both = jnp.concatenate(
        [
            jnp.concatenate([rows[f, 2 * m], nil], axis=1),
            jnp.concatenate([nil, rows[f, 2 * m + 1]], axis=1),
        ],
        axis=0,
    )
    factors = jnp.concatenate(
        [jnp.concatenate([lat[t, 2 * m], lat[t, 2 * m + 1]], axis=1) for t in tiles], axis=0
    )
    mapped = lax.dot_general(both, factors, NT, preferred_element_type=jnp.float32)
    for x, view in enumerate(views):
        part = mapped[:, x * LANES : (x + 1) * LANES]
        for q in range(4):
            view[q // 2, 16 * m : 16 * m + 16, (q % 2) * LANES : (q % 2 + 1) * LANES] = (
                jnp.concatenate([part[8 * q : 8 * q + 8], part[ROWS + 8 * q : ROWS + 8 * q + 8]])
            ).astype(jnp.bfloat16)


def multiply_fields(wide, weights, first, block, r, store):
    step = 256
    grid = jnp.dot(wide[block, r : r + step], weights(block), preferred_element_type=jnp.float32)
    here = grid[:, :LANES] * grid[:, LANES:]
    if block == 0:
        first[r : r + step] = here
        return
    low = iota((step // 8, 8, LANES), 1) < QUAD
    here = here.reshape(step // 8, 8, LANES)
    there = first[r : r + step].reshape(step // 8, 8, LANES)
    even = jnp.where(low, there, here)
    odd = pltpu.roll(jnp.where(low, here, there), QUAD, 1)
    mixed = jnp.concatenate([even[:, None], odd[:, None]], axis=1)
    store(r // QUAD, step // QUAD, mixed.reshape(step // QUAD, 8, LANES).astype(jnp.bfloat16))


def together(main, more):
    given = 0
    for n, step in enumerate(main):
        until = (n + 1) * len(more) // len(main)
        for other in more[given:until]:
            other()
        given = until
        step()


def multiply_steps(wide, weights, first, store):
    return [
        functools.partial(multiply_fields, wide, weights, first, block, r, store)
        for block in range(2)
        for r in range(0, wide.shape[1], 256)
    ]


def tile_sets(tiles):
    return [list(range(t, min(t + 2, tiles))) for t in range(0, tiles, 2)]


def order_pairs(total, orders, late):
    return [m for m in range(total // 2) if (2 * m % orders >= orders - CHUNK) == late]


def map_steps(rows, lat, views, f, tiles, pairs=None):
    return [
        functools.partial(map_rows, rows, lat, views, f, tiles, m)
        for m in (range(rows.shape[1] // 2) if pairs is None else pairs)
    ]


def butterfly_kernel(
    n_ord, n_blk, early, coef_hbm, leaf_hbm, interp_hbm, lat_hbm, ids_hbm, *refs,
):
    if early:
        rows, lat, wide, ready, done, half, *refs = refs
    else:
        rows, lat, wide, ready, *refs = refs
    (
        coef, leaf, interp, ids, own, last, came, values, first,
        coef_sem, piece_sem, leaf_sem, interp_sem, ids_sem, lat_in_sem,
        level_send, level_recv, group_send, group_recv, own_sem,
        lat_send, lat_recv, lat_pass,
    ) = refs
    me_ord, me_blk = lax.axis_index("ord"), lax.axis_index("blk")
    pieces, orders, _, parts, _, depth = coef.shape
    levels = interp.shape[0]
    per_piece = orders // CHUNK
    chunks = pieces * per_piece
    tiles = lat.shape[0]
    height = n_ord * ROWS
    total = n_ord * orders
    rank = interp.shape[-1]
    steps = chunks + LEVEL_LAG * (levels - 1)

    def coef_in(f, i, part):
        return pltpu.make_async_copy(
            coef_hbm.at[i, part, :, pl.ds(pl.multiple_of(f * FIELDS, FIELDS), FIELDS)],
            coef.at[f, i, :, part], coef_sem.at[i, part],
        )

    def piece_in(f, part):
        return pltpu.make_async_copy(
            coef_hbm.at[:, part, :, pl.ds(pl.multiple_of(f * FIELDS, FIELDS), FIELDS)],
            coef.at[f, :, :, part], piece_sem.at[f, part],
        )

    def leaf_in(i):
        return pltpu.make_async_copy(leaf_hbm.at[i], leaf.at[i], leaf_sem.at[i])

    interp_in = pltpu.make_async_copy(interp_hbm, interp, interp_sem)
    ids_in = pltpu.make_async_copy(ids_hbm, ids, ids_sem)

    def lat_rows(t, o):
        return lat.at[t, pl.ds(pl.multiple_of(o * orders, orders), orders)]

    def lat_in(t):
        return pltpu.make_async_copy(
            lat_hbm.at[:, pl.ds(t * LANES, LANES)], lat_rows(t, me_ord), lat_in_sem.at[t]
        )

    barrier = pltpu.get_barrier_semaphore()
    partners = [me_blk ^ (n_blk >> (k + 1)) for k in range(levels)]
    for k in range(levels):
        pl.semaphore_signal(barrier, inc=1, device_id={"blk": partners[k]}, device_id_type=MESH)
    for d in range(1, n_ord):
        pl.semaphore_signal(
            barrier, inc=1, device_id={"ord": lax.rem(me_ord + d, n_ord)}, device_id_type=MESH
        )

    def load_orders(begin, end):
        for i in range(begin, end):
            leaf_in(i).start()
            for part in range(parts):
                coef_in(0, i, part).start()

    load_orders(0, 2 * CHUNK)
    for t in range(tiles):
        lat_in(t).start()
    interp_in.start()

    def leaf_step(c):
        f, i = c // per_piece, lax.rem(c, per_piece) * CHUNK

        @pl.when(f == 0)
        def _():
            for h in range(CHUNK):
                leaf_in(i + h).wait()
                for part in range(parts):
                    coef_in(0, i + h, part).wait()

        @pl.when((f > 0) & (i == 0))
        def _():
            for part in range(parts):
                piece_in(f, part).wait()

        order = row_order()
        reduced = jnp.concatenate(
            [
                lax.dot_general(
                    coef[f, i + h].reshape(height, depth), leaf[i + h], NT,
                    preferred_element_type=jnp.float32,
                ).astype(jnp.bfloat16)
                for h in range(CHUNK)
            ],
            axis=1,
        )
        for r in range(0, height, 128):
            moved = jnp.dot(
                order, reduced[r : r + 128], preferred_element_type=jnp.float32
            ).astype(jnp.bfloat16)
            for h in range(CHUNK):
                own[0, c, h, r : r + 128] = moved[:, h * rank : (h + 1) * rank]

    leaf_step(0)
    pl.semaphore_wait(barrier, levels + n_ord - 1)

    def level_copy(k, c):
        return pltpu.make_async_remote_copy(
            src_ref=own.at[k, c], dst_ref=came.at[k, c],
            send_sem=level_send.at[k, c], recv_sem=level_recv.at[k, c],
            device_id={"blk": partners[k]}, device_id_type=MESH,
        )

    def landing(c):
        at = me_ord * orders + lax.rem(c, per_piece) * CHUNK
        return rows.at[c // per_piece, pl.ds(at, CHUNK)]

    def group_copy(c, d):
        peer = lax.rem(me_ord + d, n_ord)
        return pltpu.make_async_remote_copy(
            src_ref=last.at[c, peer], dst_ref=landing(c),
            send_sem=group_send.at[c, d], recv_sem=group_recv.at[c, d],
            device_id={"ord": peer}, device_id_type=MESH,
        )

    def own_copy(c):
        return pltpu.make_async_copy(last.at[c, me_ord], landing(c), own_sem.at[c])

    spans = n_ord // 2
    mate = me_ord ^ 1

    def lat_copy(d, t):
        target = mate if d == 0 else lax.rem(me_ord + 2 * d, n_ord)
        return pltpu.make_async_remote_copy(
            src_ref=lat_rows(t, me_ord), dst_ref=lat_rows(t, me_ord),
            send_sem=lat_send.at[d, t], recv_sem=lat_recv.at[d, t],
            device_id={"ord": target}, device_id_type=MESH,
        )

    def lat_forward(d, t):
        source = lax.rem(me_ord + n_ord - 2 * d, n_ord)
        return pltpu.make_async_remote_copy(
            src_ref=lat_rows(t, source), dst_ref=lat_rows(t, source),
            send_sem=lat_pass.at[d, t], recv_sem=lat_recv.at[spans + d, t],
            device_id={"ord": mate}, device_id_type=MESH,
        )

    def lat_start(t):
        lat_in(t).wait()
        for d in range(spans - 1, -1, -1):
            lat_copy(d, t).start()

    def lat_pass_on(t):
        for d in range(1, spans):
            lat_copy(d, t).wait_recv()
            lat_forward(d, t).start()

    def lat_arrived(t):
        lat_copy(0, t).wait_recv()
        for d in range(1, spans):
            lat_forward(d, t).wait_recv()

    def rows_arrived(f, begin, end):
        for n in range(begin, end):
            for d in range(1, n_ord):
                group_copy(f * per_piece + n, d).wait_recv()
            own_copy(f * per_piece + n).wait()

    level_copy(0, 0).start()
    load_orders(2 * CHUNK, orders)

    for c in range(1, WINDOW):
        leaf_step(c)
        level_copy(0, c).start()

    for f in range(1, pieces):
        for part in range(parts):
            piece_in(f, part).start()
    ids_in.start()
    for t in range(tiles):
        lat_start(t)
    interp_in.wait()

    def level_step(k, s):
        c = s - k * LEVEL_LAG

        @pl.when((c >= 0) & (c < chunks))
        def _():
            i = lax.rem(c, per_piece) * CHUNK
            level_copy(k, c).wait_recv()
            if k == 0:
                @pl.when(s + WINDOW < chunks)
                def _():
                    level_copy(0, s + WINDOW).start()

            for h in range(CHUNK):
                both = jnp.concatenate([own[k, c, h], came[k, c, h]], axis=1)
                factors = jnp.concatenate([interp[k, 0, i + h], interp[k, 1, i + h]], axis=1)
                mixed = lax.dot_general(
                    both, factors, NT, preferred_element_type=jnp.float32
                ).astype(jnp.bfloat16)
                if k + 1 < levels:
                    own[k + 1, c, h] = mixed
                else:
                    last[c, :, h] = mixed.reshape(n_ord, ROWS, rank)
            if k + 1 < levels:
                level_copy(k + 1, c).start()
            else:
                for d in range(1, n_ord):
                    group_copy(c, d).start()
                own_copy(c).start()

    begins = []
    for f in range(pieces - 1):
        begins.append(max(FIRST_UNIT + f * (tiles + 1), 2 * (f * per_piece + UNIT_DELAY - 2)))

    @pl.loop(0, max([2 * steps] + [b + tiles + 1 for b in begins]))
    def _(j):
        s = j // 2

        @pl.when(lax.rem(j, 2) == 0)
        def _():
            @pl.when(s + WINDOW < chunks)
            def _():
                leaf_step(s + WINDOW)

            level_step(0, s)

            @pl.when(s == 2)
            def _():
                ids_in.wait()
                spread_tables(ids[...], wide)
                if early:
                    half[...] = jnp.zeros(half.shape, half.dtype)

            for t in range(tiles):
                @pl.when(s == min(LAT_STEP * t + LAT_PASS, steps - 1))
                def _():
                    lat_pass_on(t)

        @pl.when(lax.rem(j, 2) == 1)
        def _():
            for k in range(1, levels):
                level_step(k, s)

        if early:
            f = sum((j >= b).astype(jnp.int32) for b in begins) - 1
            begin = begins[0]
            for before, b in zip(begins, begins[1:]):
                begin = begin + (j >= b).astype(jnp.int32) * (b - before)
            v = j - begin

            @pl.when((f >= 0) & (v <= tiles))
            def _():
                @pl.when((f == 0) & (v < tiles))
                def _():
                    lat_arrived(v)

                lanes = pl.ds(pl.multiple_of((v - 1) * LANES, LANES), LANES)

                def store(at, count, mixed):
                    where = pl.ds(at, count)
                    done[f // 2, where, :, lanes] = jnp.concatenate(
                        [half[where, :, lanes], mixed], axis=1
                    )
                    half[where, :, lanes] = mixed

                new, was = values.at[lax.rem(v, 2)], values.at[lax.rem(v + 1, 2)]

                def old(block):
                    return was[block]

                @pl.when(v == 0)
                def _():
                    rows_arrived(f, 0, per_piece)
                    for step in map_steps(rows, lat, [new], f, [v]):
                        step()

                @pl.when((v > 0) & (v < tiles))
                def _():
                    together(
                        multiply_steps(wide, old, first, store),
                        map_steps(rows, lat, [new], f, [v]),
                    )

                @pl.when(v == tiles)
                def _():
                    for step in multiply_steps(wide, old, first, store):
                        step()

    if not early:
        for t in range(tiles):
            lat_arrived(t)
    rows_arrived(pieces - 1, 0, per_piece - 1)
    for ts in tile_sets(tiles):
        views = [ready.at[t] for t in ts]
        for step in map_steps(rows, lat, views, pieces - 1, ts, order_pairs(total, orders, False)):
            step()
    rows_arrived(pieces - 1, per_piece - 1, per_piece)

    for t in range(tiles):
        for d in range(spans):
            lat_copy(d, t).wait_send()
        for d in range(1, spans):
            lat_forward(d, t).wait_send()

    @pl.loop(0, chunks)
    def _(c):
        for k in range(levels):
            level_copy(k, c).wait_send()
        for d in range(1, n_ord):
            group_copy(c, d).wait_send()


def butterfly(coefficients, leaf_factors, interpolants, latitude_factors, order_ids, n_ord, n_blk):
    orders, parts, fields, depth = coefficients.shape
    rank = leaf_factors.shape[1]
    levels = interpolants.shape[0]
    lats = latitude_factors.shape[1]
    tiles = lats // LANES
    group = fields // n_ord
    pieces = group // FIELDS
    chunks = pieces * orders // CHUNK
    total = n_ord * orders
    spans = n_ord // 2
    early = pieces > 1
    height = n_ord * ROWS
    hbm_spec = pl.BlockSpec(memory_space=pltpu.HBM)
    vmem_spec = pl.BlockSpec(memory_space=pltpu.VMEM)
    dma = pltpu.SemaphoreType.DMA
    bf16 = jnp.bfloat16
    out_shape = [
        pltpu.VMEM((pieces, total, ROWS, rank), bf16),
        pltpu.VMEM((tiles, total, LANES, rank), bf16),
        pltpu.VMEM((2, QUAD * NLON, 8 * total), bf16),
        pltpu.VMEM((tiles, 2, 8 * total, 2 * LANES), bf16),
    ]
    if early:
        out_shape += [
            pltpu.VMEM((pieces // 2, NLON, 16, lats), bf16),
            pltpu.VMEM((NLON, 8, lats), bf16),
        ]
    coefficients = coefficients.reshape(orders, parts, n_ord, group, depth)
    hold = functools.partial(pltpu.with_memory_space_constraint, memory_space=pltpu.HBM)
    return pl.pallas_call(
        functools.partial(butterfly_kernel, n_ord, n_blk, early),
        out_shape=tuple(out_shape),
        in_specs=[hbm_spec] * 5,
        out_specs=tuple([vmem_spec] * len(out_shape)),
        scratch_shapes=[
            pltpu.VMEM((pieces, orders, n_ord, parts, FIELDS, depth), bf16),
            pltpu.VMEM(leaf_factors.shape, bf16),
            pltpu.VMEM(interpolants.shape, bf16),
            pltpu.VMEM((1, total), jnp.int32),
            pltpu.VMEM((levels, chunks, CHUNK, height, rank), bf16),
            pltpu.VMEM((chunks, n_ord, CHUNK, ROWS, rank), bf16),
            pltpu.VMEM((levels, chunks, CHUNK, height, rank), bf16),
            pltpu.VMEM((2, 2, 8 * total, 2 * LANES), bf16),
            pltpu.VMEM((QUAD * NLON, LANES), jnp.float32),
            dma((orders, parts)),
            dma((pieces, parts)),
            dma((orders,)),
            dma,
            dma,
            dma((tiles,)),
            dma((levels, chunks)),
            dma((levels, chunks)),
            dma((chunks, n_ord)),
            dma((chunks, n_ord)),
            dma((chunks,)),
            dma((spans, tiles)),
            dma((2 * spans, tiles)),
            dma((spans, tiles)),
        ],
        compiler_params=pltpu.CompilerParams(
            collective_id=0, has_side_effects=True, vmem_limit_bytes=24 * MIB
        ),
        name="butterfly",
    )(
        hold(coefficients), hold(leaf_factors), hold(interpolants), hold(latitude_factors),
        hold(order_ids[None, :]),
    )


def products_kernel(early, orders, rows, lat, wide, ready, *refs):
    if early:
        done, half, out, values, first, stage, done_sem, stage_sem = refs
    else:
        out, values, first, stage, stage_sem = refs
    pieces = rows.shape[0]
    tiles = lat.shape[0]
    deep = stage.shape[2]
    pairs = out.shape[1]
    whole = pairs // deep - 1

    def done_out(h):
        return pltpu.make_async_copy(
            done.at[h], out.at[:, pl.ds(h * deep, deep)], done_sem.at[h]
        )

    def stage_out(t):
        lanes = pl.ds(t * LANES, LANES)
        return pltpu.make_async_copy(
            stage.at[t], out.at[:, pl.ds(whole * deep, deep), lanes], stage_sem.at[t]
        )

    for h in range(whole):
        done_out(h).start()

    def store_at(t):
        def store(at, count, mixed):
            where = pl.ds(at, count)
            if early:
                mixed = jnp.concatenate(
                    [half[where, :, t * LANES : (t + 1) * LANES], mixed], axis=1
                )
            stage[t, where] = mixed

        return store

    late = order_pairs(rows.shape[1], orders, True)

    def weights_of(t):
        def weights(block):
            pieces_of = []
            for m in range(rows.shape[1] // 2):
                source = values if m in late else ready
                pieces_of.append(source[t, block, 16 * m : 16 * m + 16])
            return jnp.concatenate(pieces_of, axis=0)

        return weights

    sets = tile_sets(tiles)

    def mapped(n):
        views = [values.at[t] for t in sets[n]]
        return map_steps(rows, lat, views, pieces - 1, sets[n], late)

    for step in mapped(0):
        step()
    for n, ts in enumerate(sets):
        more = mapped(n + 1) if n + 1 < len(sets) else []
        for x, t in enumerate(ts):
            begin, end = x * len(more) // len(ts), (x + 1) * len(more) // len(ts)
            together(multiply_steps(wide, weights_of(t), first, store_at(t)), more[begin:end])
            stage_out(t).start()

    for h in range(whole):
        done_out(h).wait()
    for t in range(tiles):
        stage_out(t).wait()


def products_of(orders, rows, lat, wide, ready, *more):
    pieces, total, _, rank = rows.shape
    tiles = lat.shape[0]
    early = len(more) > 0
    pairs = pieces * FIELDS // 2
    deep = 16 if early else 8
    dma = pltpu.SemaphoreType.DMA
    scratch = [
        pltpu.VMEM((tiles, 2, 8 * total, 2 * LANES), jnp.bfloat16),
        pltpu.VMEM((QUAD * NLON, LANES), jnp.float32),
        pltpu.VMEM((tiles, NLON, deep, LANES), jnp.bfloat16),
    ]
    if early:
        scratch.append(dma((max(pairs // deep - 1, 1),)))
    scratch.append(dma((tiles,)))
    operands = [
        pltpu.with_memory_space_constraint(x, memory_space=pltpu.VMEM)
        for x in (rows, lat, wide, ready, *more)
    ]
    return pl.pallas_call(
        functools.partial(products_kernel, early, orders),
        out_shape=jax.ShapeDtypeStruct((NLON, pairs, tiles * LANES), jnp.bfloat16),
        in_specs=[pl.BlockSpec(memory_space=pltpu.VMEM)] * len(operands),
        out_specs=pl.BlockSpec(memory_space=pl.ANY),
        scratch_shapes=scratch,
        compiler_params=pltpu.CompilerParams(vmem_limit_bytes=14 * MIB),
        name="products",
    )(*operands)


def per_device(coefficients, leaf_factors, level_interpolants, latitude_factors, order_ids):
    return products_of(
        coefficients.shape[0],
        *butterfly(
            coefficients, leaf_factors, level_interpolants, latitude_factors, order_ids,
            lax.axis_size("ord"), lax.axis_size("blk"),
        )
    )


def solution(mesh):
    in_specs = (
        P("ord", None, None, "blk"),
        P("ord", None, "blk"),
        P(None, None, "ord", None, "blk"),
        P("ord", "blk", None),
        P(),
    )
    out_specs = P(None, "ord", "blk")
    return jax.shard_map(
        per_device, mesh=mesh, in_specs=in_specs, out_specs=out_specs, check_vma=False
    )
```

```python
import functools
import math

import jax
import jax.numpy as jnp
from jax import lax
from jax.experimental import pallas as pl
from jax.experimental.pallas import tpu as pltpu
from jax.sharding import PartitionSpec as P

PERIOD = 16384
NLON = 256
LANES = 128
FIELDS = 16
ROWS = 2 * FIELDS
QUAD = 4
CHUNK = 2
WINDOW = 2
LEVEL_LAG = 2
FIRST_UNIT = 22
UNIT_DELAY = 11
LAT_STEP = 2
LAT_PASS = 4
MIB = 2**20
MESH = pl.DeviceIdType.MESH
NT = (((1,), (1,)), ((), ()))


def iota(shape, dimension):
    return lax.broadcasted_iota(jnp.int32, shape, dimension)


def synthesis_table(order_ids, count, period):
    steps = iota((count, order_ids.shape[1]), 0)
    phase = lax.rem(steps * order_ids, period).astype(jnp.float32) * (2.0 * math.pi / period)
    weight = jnp.where(order_ids == 0, 1.0, 2.0).astype(jnp.float32)
    table = jnp.concatenate([weight * jnp.cos(phase), -weight * jnp.sin(phase)], axis=1)
    return table.astype(jnp.bfloat16)


def spread_tables(order_ids, wide_ref):
    total = order_ids.shape[1]
    table = synthesis_table(order_ids, NLON, PERIOD)
    tall, broad = wide_ref.shape[1:]
    row, column = iota((2 * total, broad), 0), iota((2 * total, broad), 1)
    source = ((column >> 2) & 1) * total + (column >> 3)
    columns = (row == source).astype(jnp.float32).astype(jnp.bfloat16)
    step = min(tall, 256)
    for side in range(2):
        for r in range(0, tall, step):
            row, lon = iota((step, NLON), 0) + r, iota((step, NLON), 1)
            rows = (((row >> 2) ^ side) == lon).astype(jnp.float32).astype(jnp.bfloat16)
            some = jnp.dot(rows, table, preferred_element_type=jnp.float32).astype(jnp.bfloat16)
            most = jnp.dot(some, columns, preferred_element_type=jnp.float32)
            keep = (iota((step, broad), 0) & 3) == (iota((step, broad), 1) & 3)
            wide_ref[side, pl.ds(r, step), :] = jnp.where(keep, most, 0.0).astype(jnp.bfloat16)


def row_order():
    size = 128
    to, come = iota((size, size), 0), iota((size, size), 1)
    inside = to & 31
    block, parity, part, pair = inside >> 4, (inside >> 3) & 1, (inside >> 2) & 1, inside & 3
    source = (to - inside) + part * FIELDS + block * 8 + pair * 2 + parity
    return (source == come).astype(jnp.float32).astype(jnp.bfloat16)


def map_rows(rows, lat, views, f, tiles, m):
    nil = jnp.zeros((ROWS, rows.shape[3]), jnp.bfloat16)
    both = jnp.concatenate(
        [
            jnp.concatenate([rows[f, 2 * m], nil], axis=1),
            jnp.concatenate([nil, rows[f, 2 * m + 1]], axis=1),
        ],
        axis=0,
    )
    factors = jnp.concatenate(
        [jnp.concatenate([lat[t, 2 * m], lat[t, 2 * m + 1]], axis=1) for t in tiles], axis=0
    )
    mapped = lax.dot_general(both, factors, NT, preferred_element_type=jnp.float32)
    for x, view in enumerate(views):
        part = mapped[:, x * LANES : (x + 1) * LANES]
        for q in range(4):
            view[q // 2, 16 * m : 16 * m + 16, (q % 2) * LANES : (q % 2 + 1) * LANES] = (
                jnp.concatenate([part[8 * q : 8 * q + 8], part[ROWS + 8 * q : ROWS + 8 * q + 8]])
            ).astype(jnp.bfloat16)


def multiply_fields(wide, weights, first, block, r, store):
    step = 256
    grid = jnp.dot(wide[block, r : r + step], weights(block), preferred_element_type=jnp.float32)
    here = grid[:, :LANES] * grid[:, LANES:]
    if block == 0:
        first[r : r + step] = here
        return
    low = iota((step // 8, 8, LANES), 1) < QUAD
    here = here.reshape(step // 8, 8, LANES)
    there = first[r : r + step].reshape(step // 8, 8, LANES)
    even = jnp.where(low, there, here)
    odd = pltpu.roll(jnp.where(low, here, there), QUAD, 1)
    mixed = jnp.concatenate([even[:, None], odd[:, None]], axis=1)
    store(r // QUAD, step // QUAD, mixed.reshape(step // QUAD, 8, LANES).astype(jnp.bfloat16))


def together(main, more):
    given = 0
    for n, step in enumerate(main):
        until = (n + 1) * len(more) // len(main)
        for other in more[given:until]:
            other()
        given = until
        step()


def multiply_steps(wide, weights, first, store):
    return [
        functools.partial(multiply_fields, wide, weights, first, block, r, store)
        for block in range(2)
        for r in range(0, wide.shape[1], 256)
    ]


def tile_sets(tiles):
    return [list(range(t, min(t + 2, tiles))) for t in range(0, tiles, 2)]


def order_pairs(total, orders, late):
    return [m for m in range(total // 2) if (2 * m % orders >= orders - CHUNK) == late]


def map_steps(rows, lat, views, f, tiles, pairs=None):
    return [
        functools.partial(map_rows, rows, lat, views, f, tiles, m)
        for m in (range(rows.shape[1] // 2) if pairs is None else pairs)
    ]


def butterfly_kernel(
    n_ord, n_blk, early, coef_hbm, leaf_hbm, interp_hbm, lat_hbm, ids_hbm, *refs,
):
    if early:
        rows, lat, wide, ready, done, half, *refs = refs
    else:
        rows, lat, wide, ready, *refs = refs
    (
        coef, leaf, interp, ids, own, last, came, values, first,
        coef_sem, piece_sem, leaf_sem, interp_sem, ids_sem, lat_in_sem,
        level_send, level_recv, group_send, group_recv, own_sem,
        lat_send, lat_recv, lat_pass,
    ) = refs
    me_ord, me_blk = lax.axis_index("ord"), lax.axis_index("blk")
    pieces, orders, _, parts, _, depth = coef.shape
    levels = interp.shape[0]
    per_piece = orders // CHUNK
    chunks = pieces * per_piece
    tiles = lat.shape[0]
    height = n_ord * ROWS
    total = n_ord * orders
    rank = interp.shape[-1]
    steps = chunks + LEVEL_LAG * (levels - 1)

    def coef_in(f, i, part):
        return pltpu.make_async_copy(
            coef_hbm.at[i, part, :, pl.ds(pl.multiple_of(f * FIELDS, FIELDS), FIELDS)],
            coef.at[f, i, :, part], coef_sem.at[i, part],
        )

    def piece_in(f, part):
        return pltpu.make_async_copy(
            coef_hbm.at[:, part, :, pl.ds(pl.multiple_of(f * FIELDS, FIELDS), FIELDS)],
            coef.at[f, :, :, part], piece_sem.at[f, part],
        )

    def leaf_in(i):
        return pltpu.make_async_copy(leaf_hbm.at[i], leaf.at[i], leaf_sem.at[i])

    interp_in = pltpu.make_async_copy(interp_hbm, interp, interp_sem)
    ids_in = pltpu.make_async_copy(ids_hbm, ids, ids_sem)

    def lat_rows(t, o):
        return lat.at[t, pl.ds(pl.multiple_of(o * orders, orders), orders)]

    def lat_in(t):
        return pltpu.make_async_copy(
            lat_hbm.at[:, pl.ds(t * LANES, LANES)], lat_rows(t, me_ord), lat_in_sem.at[t]
        )

    barrier = pltpu.get_barrier_semaphore()
    partners = [me_blk ^ (n_blk >> (k + 1)) for k in range(levels)]
    for k in range(levels):
        pl.semaphore_signal(barrier, inc=1, device_id={"blk": partners[k]}, device_id_type=MESH)
    for d in range(1, n_ord):
        pl.semaphore_signal(
            barrier, inc=1, device_id={"ord": lax.rem(me_ord + d, n_ord)}, device_id_type=MESH
        )

    def load_orders(begin, end):
        for i in range(begin, end):
            leaf_in(i).start()
            for part in range(parts):
                coef_in(0, i, part).start()

    load_orders(0, 2 * CHUNK)
    for t in range(tiles):
        lat_in(t).start()
    interp_in.start()

    def leaf_step(c):
        f, i = c // per_piece, lax.rem(c, per_piece) * CHUNK

        @pl.when(f == 0)
        def _():
            for h in range(CHUNK):
                leaf_in(i + h).wait()
                for part in range(parts):
                    coef_in(0, i + h, part).wait()

        @pl.when((f > 0) & (i == 0))
        def _():
            for part in range(parts):
                piece_in(f, part).wait()

        order = row_order()
        reduced = jnp.concatenate(
            [
                lax.dot_general(
                    coef[f, i + h].reshape(height, depth), leaf[i + h], NT,
                    preferred_element_type=jnp.float32,
                ).astype(jnp.bfloat16)
                for h in range(CHUNK)
            ],
            axis=1,
        )
        for r in range(0, height, 128):
            moved = jnp.dot(
                order, reduced[r : r + 128], preferred_element_type=jnp.float32
            ).astype(jnp.bfloat16)
            for h in range(CHUNK):
                own[0, c, h, r : r + 128] = moved[:, h * rank : (h + 1) * rank]

    leaf_step(0)
    pl.semaphore_wait(barrier, levels + n_ord - 1)

    def level_copy(k, c):
        return pltpu.make_async_remote_copy(
            src_ref=own.at[k, c], dst_ref=came.at[k, c],
            send_sem=level_send.at[k, c], recv_sem=level_recv.at[k, c],
            device_id={"blk": partners[k]}, device_id_type=MESH,
        )

    def landing(c):
        at = me_ord * orders + lax.rem(c, per_piece) * CHUNK
        return rows.at[c // per_piece, pl.ds(at, CHUNK)]

    def group_copy(c, d):
        peer = lax.rem(me_ord + d, n_ord)
        return pltpu.make_async_remote_copy(
            src_ref=last.at[c, peer], dst_ref=landing(c),
            send_sem=group_send.at[c, d], recv_sem=group_recv.at[c, d],
            device_id={"ord": peer}, device_id_type=MESH,
        )

    def own_copy(c):
        return pltpu.make_async_copy(last.at[c, me_ord], landing(c), own_sem.at[c])

    spans = n_ord // 2
    mate = me_ord ^ 1

    def lat_copy(d, t):
        target = mate if d == 0 else lax.rem(me_ord + 2 * d, n_ord)
        return pltpu.make_async_remote_copy(
            src_ref=lat_rows(t, me_ord), dst_ref=lat_rows(t, me_ord),
            send_sem=lat_send.at[d, t], recv_sem=lat_recv.at[d, t],
            device_id={"ord": target}, device_id_type=MESH,
        )

    def lat_forward(d, t):
        source = lax.rem(me_ord + n_ord - 2 * d, n_ord)
        return pltpu.make_async_remote_copy(
            src_ref=lat_rows(t, source), dst_ref=lat_rows(t, source),
            send_sem=lat_pass.at[d, t], recv_sem=lat_recv.at[spans + d, t],
            device_id={"ord": mate}, device_id_type=MESH,
        )

    def lat_start(t):
        lat_in(t).wait()
        for d in range(spans - 1, -1, -1):
            lat_copy(d, t).start()

    def lat_pass_on(t):
        for d in range(1, spans):
            lat_copy(d, t).wait_recv()
            lat_forward(d, t).start()

    def lat_arrived(t):
        lat_copy(0, t).wait_recv()
        for d in range(1, spans):
            lat_forward(d, t).wait_recv()

    def rows_arrived(f, begin, end):
        for n in range(begin, end):
            for d in range(1, n_ord):
                group_copy(f * per_piece + n, d).wait_recv()
            own_copy(f * per_piece + n).wait()

    level_copy(0, 0).start()

    for c in range(1, WINDOW):
        leaf_step(c)
        level_copy(0, c).start()

    load_orders(2 * CHUNK, orders)
    for t in range(tiles):
        lat_start(t)
    ids_in.start()
    for f in range(1, pieces):
        for part in range(parts):
            piece_in(f, part).start()
    interp_in.wait()

    def level_step(k, s):
        c = s - k * LEVEL_LAG

        @pl.when((c >= 0) & (c < chunks))
        def _():
            i = lax.rem(c, per_piece) * CHUNK
            level_copy(k, c).wait_recv()
            if k == 0:
                @pl.when(s + WINDOW < chunks)
                def _():
                    level_copy(0, s + WINDOW).start()

            for h in range(CHUNK):
                both = jnp.concatenate([own[k, c, h], came[k, c, h]], axis=1)
                factors = jnp.concatenate([interp[k, 0, i + h], interp[k, 1, i + h]], axis=1)
                mixed = lax.dot_general(
                    both, factors, NT, preferred_element_type=jnp.float32
                ).astype(jnp.bfloat16)
                if k + 1 < levels:
                    own[k + 1, c, h] = mixed
                else:
                    last[c, :, h] = mixed.reshape(n_ord, ROWS, rank)
            if k + 1 < levels:
                level_copy(k + 1, c).start()
            else:
                for d in sorted(range(1, n_ord), key=lambda d: abs(d - spans)):
                    group_copy(c, d).start()
                own_copy(c).start()

    begins = []
    for f in range(pieces - 1):
        begins.append(max(FIRST_UNIT + f * (tiles + 1), 2 * (f * per_piece + UNIT_DELAY - 2)))

    @pl.loop(0, max([2 * steps] + [b + tiles + 1 for b in begins]))
    def _(j):
        s = j // 2

        @pl.when(lax.rem(j, 2) == 0)
        def _():
            @pl.when(s + WINDOW < chunks)
            def _():
                leaf_step(s + WINDOW)

            level_step(0, s)

            @pl.when(s == 2)
            def _():
                ids_in.wait()
                spread_tables(ids[...], wide)
                if early:
                    half[...] = jnp.zeros(half.shape, half.dtype)

            for t in range(tiles):
                @pl.when(s == min(LAT_STEP * t + LAT_PASS, steps - 1))
                def _():
                    lat_pass_on(t)

        @pl.when(lax.rem(j, 2) == 1)
        def _():
            for k in range(1, levels):
                level_step(k, s)

        if early:
            f = sum((j >= b).astype(jnp.int32) for b in begins) - 1
            begin = begins[0]
            for before, b in zip(begins, begins[1:]):
                begin = begin + (j >= b).astype(jnp.int32) * (b - before)
            v = j - begin

            @pl.when((f >= 0) & (v <= tiles))
            def _():
                @pl.when((f == 0) & (v < tiles))
                def _():
                    lat_arrived(v)

                lanes = pl.ds(pl.multiple_of((v - 1) * LANES, LANES), LANES)

                def store(at, count, mixed):
                    where = pl.ds(at, count)
                    done[f // 2, where, :, lanes] = jnp.concatenate(
                        [half[where, :, lanes], mixed], axis=1
                    )
                    half[where, :, lanes] = mixed

                new, was = values.at[lax.rem(v, 2)], values.at[lax.rem(v + 1, 2)]

                def old(block):
                    return was[block]

                @pl.when(v == 0)
                def _():
                    rows_arrived(f, 0, per_piece)
                    for step in map_steps(rows, lat, [new], f, [v]):
                        step()

                @pl.when((v > 0) & (v < tiles))
                def _():
                    together(
                        multiply_steps(wide, old, first, store),
                        map_steps(rows, lat, [new], f, [v]),
                    )

                @pl.when(v == tiles)
                def _():
                    for step in multiply_steps(wide, old, first, store):
                        step()

    if not early:
        for t in range(tiles):
            lat_arrived(t)
    rows_arrived(pieces - 1, 0, per_piece - 1)
    for ts in tile_sets(tiles):
        views = [ready.at[t] for t in ts]
        for step in map_steps(rows, lat, views, pieces - 1, ts, order_pairs(total, orders, False)):
            step()
    rows_arrived(pieces - 1, per_piece - 1, per_piece)

    for t in range(tiles):
        for d in range(spans):
            lat_copy(d, t).wait_send()
        for d in range(1, spans):
            lat_forward(d, t).wait_send()

    @pl.loop(0, chunks)
    def _(c):
        for k in range(levels):
            level_copy(k, c).wait_send()
        for d in range(1, n_ord):
            group_copy(c, d).wait_send()


def butterfly(coefficients, leaf_factors, interpolants, latitude_factors, order_ids, n_ord, n_blk):
    orders, parts, fields, depth = coefficients.shape
    rank = leaf_factors.shape[1]
    levels = interpolants.shape[0]
    lats = latitude_factors.shape[1]
    tiles = lats // LANES
    group = fields // n_ord
    pieces = group // FIELDS
    chunks = pieces * orders // CHUNK
    total = n_ord * orders
    spans = n_ord // 2
    early = pieces > 1
    height = n_ord * ROWS
    hbm_spec = pl.BlockSpec(memory_space=pltpu.HBM)
    vmem_spec = pl.BlockSpec(memory_space=pltpu.VMEM)
    dma = pltpu.SemaphoreType.DMA
    bf16 = jnp.bfloat16
    out_shape = [
        pltpu.VMEM((pieces, total, ROWS, rank), bf16),
        pltpu.VMEM((tiles, total, LANES, rank), bf16),
        pltpu.VMEM((2, QUAD * NLON, 8 * total), bf16),
        pltpu.VMEM((tiles, 2, 8 * total, 2 * LANES), bf16),
    ]
    if early:
        out_shape += [
            pltpu.VMEM((pieces // 2, NLON, 16, lats), bf16),
            pltpu.VMEM((NLON, 8, lats), bf16),
        ]
    coefficients = coefficients.reshape(orders, parts, n_ord, group, depth)
    hold = functools.partial(pltpu.with_memory_space_constraint, memory_space=pltpu.HBM)
    return pl.pallas_call(
        functools.partial(butterfly_kernel, n_ord, n_blk, early),
        out_shape=tuple(out_shape),
        in_specs=[hbm_spec] * 5,
        out_specs=tuple([vmem_spec] * len(out_shape)),
        scratch_shapes=[
            pltpu.VMEM((pieces, orders, n_ord, parts, FIELDS, depth), bf16),
            pltpu.VMEM(leaf_factors.shape, bf16),
            pltpu.VMEM(interpolants.shape, bf16),
            pltpu.VMEM((1, total), jnp.int32),
            pltpu.VMEM((levels, chunks, CHUNK, height, rank), bf16),
            pltpu.VMEM((chunks, n_ord, CHUNK, ROWS, rank), bf16),
            pltpu.VMEM((levels, chunks, CHUNK, height, rank), bf16),
            pltpu.VMEM((2, 2, 8 * total, 2 * LANES), bf16),
            pltpu.VMEM((QUAD * NLON, LANES), jnp.float32),
            dma((orders, parts)),
            dma((pieces, parts)),
            dma((orders,)),
            dma,
            dma,
            dma((tiles,)),
            dma((levels, chunks)),
            dma((levels, chunks)),
            dma((chunks, n_ord)),
            dma((chunks, n_ord)),
            dma((chunks,)),
            dma((spans, tiles)),
            dma((2 * spans, tiles)),
            dma((spans, tiles)),
        ],
        compiler_params=pltpu.CompilerParams(
            collective_id=0, has_side_effects=True, vmem_limit_bytes=24 * MIB
        ),
        name="butterfly",
    )(
        hold(coefficients), hold(leaf_factors), hold(interpolants), hold(latitude_factors),
        hold(order_ids[None, :]),
    )


def products_kernel(early, orders, rows, lat, wide, ready, *refs):
    if early:
        done, half, out, values, first, stage, done_sem, stage_sem = refs
    else:
        out, values, first, stage, stage_sem = refs
    pieces = rows.shape[0]
    tiles = lat.shape[0]
    deep = stage.shape[2]
    pairs = out.shape[1]
    whole = pairs // deep - 1

    def done_out(h):
        return pltpu.make_async_copy(
            done.at[h], out.at[:, pl.ds(h * deep, deep)], done_sem.at[h]
        )

    def stage_out(t):
        lanes = pl.ds(t * LANES, LANES)
        return pltpu.make_async_copy(
            stage.at[t], out.at[:, pl.ds(whole * deep, deep), lanes], stage_sem.at[t]
        )

    for h in range(whole):
        done_out(h).start()

    def store_at(t):
        def store(at, count, mixed):
            where = pl.ds(at, count)
            if early:
                mixed = jnp.concatenate(
                    [half[where, :, t * LANES : (t + 1) * LANES], mixed], axis=1
                )
            stage[t, where] = mixed

        return store

    late = order_pairs(rows.shape[1], orders, True)

    def weights_of(t):
        def weights(block):
            pieces_of = []
            for m in range(rows.shape[1] // 2):
                source = values if m in late else ready
                pieces_of.append(source[t, block, 16 * m : 16 * m + 16])
            return jnp.concatenate(pieces_of, axis=0)

        return weights

    sets = tile_sets(tiles)

    def mapped(n):
        views = [values.at[t] for t in sets[n]]
        return map_steps(rows, lat, views, pieces - 1, sets[n], late)

    for step in mapped(0):
        step()
    for n, ts in enumerate(sets):
        more = mapped(n + 1) if n + 1 < len(sets) else []
        for x, t in enumerate(ts):
            begin, end = x * len(more) // len(ts), (x + 1) * len(more) // len(ts)
            together(multiply_steps(wide, weights_of(t), first, store_at(t)), more[begin:end])
            stage_out(t).start()

    for h in range(whole):
        done_out(h).wait()
    for t in range(tiles):
        stage_out(t).wait()


def products_of(orders, rows, lat, wide, ready, *more):
    pieces, total, _, rank = rows.shape
    tiles = lat.shape[0]
    early = len(more) > 0
    pairs = pieces * FIELDS // 2
    deep = 16 if early else 8
    dma = pltpu.SemaphoreType.DMA
    scratch = [
        pltpu.VMEM((tiles, 2, 8 * total, 2 * LANES), jnp.bfloat16),
        pltpu.VMEM((QUAD * NLON, LANES), jnp.float32),
        pltpu.VMEM((tiles, NLON, deep, LANES), jnp.bfloat16),
    ]
    if early:
        scratch.append(dma((max(pairs // deep - 1, 1),)))
    scratch.append(dma((tiles,)))
    operands = [
        pltpu.with_memory_space_constraint(x, memory_space=pltpu.VMEM)
        for x in (rows, lat, wide, ready, *more)
    ]
    return pl.pallas_call(
        functools.partial(products_kernel, early, orders),
        out_shape=jax.ShapeDtypeStruct((NLON, pairs, tiles * LANES), jnp.bfloat16),
        in_specs=[pl.BlockSpec(memory_space=pltpu.VMEM)] * len(operands),
        out_specs=pl.BlockSpec(memory_space=pl.ANY),
        scratch_shapes=scratch,
        compiler_params=pltpu.CompilerParams(vmem_limit_bytes=14 * MIB),
        name="products",
    )(*operands)


def per_device(coefficients, leaf_factors, level_interpolants, latitude_factors, order_ids):
    return products_of(
        coefficients.shape[0],
        *butterfly(
            coefficients, leaf_factors, level_interpolants, latitude_factors, order_ids,
            lax.axis_size("ord"), lax.axis_size("blk"),
        )
    )


def solution(mesh):
    in_specs = (
        P("ord", None, None, "blk"),
        P("ord", None, "blk"),
        P(None, None, "ord", None, "blk"),
        P("ord", "blk", None),
        P(),
    )
    out_specs = P(None, "ord", "blk")
    return jax.shard_map(
        per_device, mesh=mesh, in_specs=in_specs, out_specs=out_specs, check_vma=False
    )
```
